256 devices in a mesh: rows: 32 (over z, x), cols: 8 (over y, core).
Axes of the slice: x: 4, y: 4, z: 8, core: 2. Of those that a mesh axis runs over, the one named last changes fastest.
Arguments:
- features: bfloat16 [256, 256, 512], P('rows', 'cols'), may hold values from -6 to 6
- kernel: bfloat16 [4608, 512], replicated, may hold values from -0.09375 to 0.09375
- out_grad: bfloat16 [256, 256, 512], P('rows', 'cols'), may hold values from -6 to 6
- projector: bfloat16 [4096, 2048], P('rows', 'cols'), may hold values from -0.375 to 0.375
- mixers: bfloat16 [2, 128, 256], replicated, may hold values from -0.5 to 0.5
Outputs:
- output: bfloat16 [256, 256, 512], P('rows', 'cols')
- grad_features: bfloat16 [256, 256, 512], P('rows', 'cols')
- grad_kernel: float32 [9, 512, 512], P(None, 'rows', 'cols')
- sketch: bfloat16 [128, 4608], P('cols', 'rows')
The draws below stay inside these ranges and needn't reach their ends.
All inputs are finite; a program needn't handle non-finite values.
Results may differ from the reference program's by a relative error of at most 0.015.
Values may be sent and summed in bfloat16 or wider, within the bound.
A program may use at most 192 MiB of HBM per device.

```python
import jax
import jax.numpy as jnp
from jax import lax

CH = 512
RANK = 128
NS_STEPS = 5
PATCH = 4608
PIX_DEV = 256
HEIGHT = 256
WIDTH = 256
ROW_LEVELS = 5
COL_LEVELS = 3
N_ROWS = 32
N_COLS = 8


def spiked(array, stream_key, source, target, parts, factor):
    owner, partner = [(jnp.arange(array.shape[dim]) // (array.shape[dim] // parts)).reshape([-1 if axis == dim else 1 for axis in range(array.ndim)]) for dim in (source, target)]
    chosen = jax.random.permutation(stream_key, parts)[partner]
    strong = (owner == chosen) | (owner == (partner + parts // 2) % parts)
    return jnp.where(strong, factor * array, array)


def shard_levels(key, shape, pieces, low, top_value):
    def one(axis_at, blocks):
        draws = jax.random.uniform(jax.random.fold_in(jax.random.fold_in(key, 6), axis_at), (blocks,), jnp.float32, low / len(pieces), top_value / len(pieces))
        return jnp.repeat(jnp.exp(draws), shape[axis_at] // blocks).reshape((-1,) + (1,) * (len(shape) - axis_at - 1))

    gain = one(*pieces[0])
    for cut in pieces[1:]:
        gain = gain * one(*cut)
    return gain


def noise(rng, shape, width, most, cuts=(), kind=jnp.bfloat16):
    result = width * jax.random.normal(rng, shape, jnp.float32)
    if cuts:
        result = result * shard_levels(rng, shape, cuts, -0.22, 0.18)
    return jnp.clip(result, -most, most).astype(kind)


def gaussian_with(stream_key, shape, deviation, most, shards, heavy, held_as=jnp.bfloat16):
    drawn = deviation * jax.random.normal(stream_key, shape, jnp.float32)
    if shards:
        drawn = drawn * shard_levels(stream_key, shape, shards, -0.22, 0.18)
    return jnp.clip(spiked(drawn, jax.random.fold_in(stream_key, 3), *heavy), -most, most).astype(held_as)


def setup_inputs(seed: int = 0) -> dict:
    streams_of = jax.random.split(jax.random.key(seed), 6)
    return {
        "features": noise(streams_of[0], (HEIGHT, WIDTH, CH), 1.0, 6.0, ((0, 32), (1, 8))),
        "kernel": noise(streams_of[1], (PATCH, CH), PATCH ** -0.5, 0.09375),
        "out_grad": gaussian_with(streams_of[2], (HEIGHT, WIDTH, CH), 1.0, 6.0, ((0, 32), (1, 8)), (0, 2, 32, 2.75)),
        "projector": noise(streams_of[3], (RANK * N_ROWS, PIX_DEV * N_COLS), PIX_DEV ** -0.5, 0.375, ((0, 32), (1, 8))),
        "mixers": noise(streams_of[4], (2, RANK, 2 * RANK), RANK ** -0.5, 0.5),
    }


def finish_merge(gram_matrix, stacked, mix_matrix):
    size_two = gram_matrix.shape[0]
    identity = jnp.eye(size_two, dtype=jnp.float32)
    spread = gram_matrix / (jnp.trace(gram_matrix) + 1e-06) - identity / size_two
    spread = spread / (jnp.sqrt(jnp.sum(spread * spread)) + 1e-06)
    for sweep in range(NS_STEPS):
        square = jnp.dot(spread, spread, precision=lax.Precision.HIGHEST)
        spread = 1.5 * spread - 0.5 * jnp.dot(spread, square, precision=lax.Precision.HIGHEST)
    keeper = 0.5 * (identity + spread)
    combiner = jnp.dot(mix_matrix.astype(jnp.float32), keeper, precision=lax.Precision.HIGHEST).astype(jnp.bfloat16)
    return jnp.dot(combiner, stacked, preferred_element_type=jnp.float32).astype(jnp.bfloat16)

def full_merge(upper_part, lower_part, mix_matrix):
    stacked = jnp.concatenate([upper_part, lower_part], axis=0)
    gram_matrix = lax.dot_general(stacked, stacked, (((1,), (1,)), ((), ())), preferred_element_type=jnp.float32)
    return finish_merge(gram_matrix, stacked, mix_matrix)

def reference(features, kernel, out_grad, projector, mixers):
    height, width_all, channels = features.shape
    band_rows = height // N_ROWS
    band_cols = width_all // N_COLS
    padded = jnp.pad(features, ((1, 1), (1, 1), (0, 0)))
    grad_padded = jnp.pad(out_grad, ((1, 1), (1, 1), (0, 0)))
    taps = kernel.reshape(9, channels, channels)
    flat_grad = out_grad.reshape(-1, channels)
    block_proj = projector.reshape(N_ROWS, RANK, N_COLS, band_rows * band_cols).astype(jnp.float32)
    forward = jnp.zeros((height * width_all, channels), jnp.float32)
    backward = jnp.zeros((height * width_all, channels), jnp.float32)
    kernel_grads = []
    sketch_parts = []
    for tap_index in range(9):
        row_tap = tap_index // 3
        col_tap = tap_index % 3
        shifted = padded[row_tap:row_tap + height, col_tap:col_tap + width_all, :]
        flat_shift = shifted.reshape(-1, channels)
        forward = forward + jnp.dot(flat_shift, taps[tap_index], preferred_element_type=jnp.float32)
        grad_shift = grad_padded[2 - row_tap:2 - row_tap + height, 2 - col_tap:2 - col_tap + width_all, :].reshape(-1, channels)
        backward = backward + jnp.dot(grad_shift, taps[tap_index].T, preferred_element_type=jnp.float32)
        kernel_grads.append(lax.dot_general(flat_shift, flat_grad, (((0,), (0,)), ((), ())), preferred_element_type=jnp.float32))
        blocks = shifted.reshape(N_ROWS, band_rows, N_COLS, band_cols, channels).transpose(0, 2, 1, 3, 4)
        blocks = blocks.reshape(N_ROWS, N_COLS, band_rows * band_cols, channels).astype(jnp.float32)
        sketch_parts.append(jnp.einsum('rlcp,rcpi->rcli', block_proj, blocks, precision=lax.Precision.HIGHEST))
    output = forward.astype(jnp.bfloat16).reshape(height, width_all, channels)
    grad_features = backward.astype(jnp.bfloat16).reshape(height, width_all, channels)
    grad_kernel = jnp.stack(kernel_grads, axis=0)
    sketches = jnp.concatenate(sketch_parts, axis=3).astype(jnp.bfloat16)
    merge_grid = jax.vmap(jax.vmap(full_merge, in_axes=(0, 0, None)), in_axes=(0, 0, None))
    for tree_level in range(ROW_LEVELS):
        sketches = merge_grid(sketches[0::2], sketches[1::2], mixers[0])
    bands = sketches[0]
    merge_line = jax.vmap(full_merge, in_axes=(0, 0, None))
    for tree_level in range(COL_LEVELS):
        bands = merge_line(bands[0::2], bands[1::2], mixers[1])
    return (output, grad_features, grad_kernel, bands[0])
```

```python
import jax
import jax.numpy as jnp
from jax import lax
from jax.experimental import pallas as pl
from jax.experimental.pallas import tpu as pltpu
from jax.sharding import PartitionSpec as P

NS_STEPS = 5
NX, NZ, NY, NC = 4, 8, 4, 2
LANES = 128
CH = 512
RANK = 128
TAPS = 9
QUART = 1152
MESH = pl.DeviceIdType.MESH
F32 = jnp.float32
BF16 = jnp.bfloat16


def dot(a, b):
    return jnp.dot(a, b, preferred_element_type=F32)


def dot_t(a, b):
    return lax.dot_general(a, b, (((1,), (1,)), ((), ())), preferred_element_type=F32)


def split(v):
    high = v.astype(BF16)
    return high, (v - high.astype(F32)).astype(BF16)


def local_kernel(xs, gs, ogt, kern, out, gfeat, wt, acc_o, acc_g, xsp):
    t = pl.program_id(0)

    @pl.when(t == 0)
    def _():
        acc_o[...] = jnp.zeros_like(acc_o)
        acc_g[...] = jnp.zeros_like(acc_g)
        ci = lax.broadcasted_iota(jnp.int32, (CH, CH), 0)
        to = lax.broadcasted_iota(jnp.int32, (CH, CH), 1)
        source = lax.rem(lax.div(to, 16), NZ) * 64 + lax.div(to, 128) * 16 + lax.rem(to, 16)
        perm = jnp.where(ci == source, 1.0, 0.0).astype(BF16)
        for b in range(3):
            xsp[b] = dot(xs[b], perm).astype(BF16)

    a = lax.div(t, 3)
    b = lax.rem(t, 3)
    start = pl.multiple_of(a * 32, 32)
    back = pl.multiple_of((2 - a) * 32, 32)
    weights = kern[0]
    acc_o[...] += dot(xs[b, pl.ds(start, 256), :], weights)
    acc_g[...] += dot_t(gs[2 - b, pl.ds(back, 256), :], weights)
    terms = dot(ogt[...], xsp[b, pl.ds(start, 256), :]).astype(BF16)
    for y in range(NY):
        for core in range(NC):
            for x in range(NX):
                at = (y * NC + core) * 64
                wt[y, core, x, 0] = terms[at : at + 64, x * LANES : (x + 1) * LANES]

    @pl.when(t == TAPS - 1)
    def _():
        out[...] = acc_o[...].astype(BF16)
        gfeat[...] = acc_g[...].astype(BF16)


def local_call(xs, gs, ogt, kernel):
    whole = lambda *shape: pl.BlockSpec(shape, lambda t: (0,) * len(shape))
    return pl.pallas_call(
        local_kernel,
        grid=(TAPS,),
        in_specs=[
            whole(3, 320, CH),
            whole(3, 320, CH),
            whole(CH, 256),
            pl.BlockSpec((1, CH, CH), lambda t: (t, 0, 0)),
        ],
        out_specs=[
            whole(256, CH),
            whole(256, CH),
            pl.BlockSpec((NY, NC, NX, 1, 64, LANES), lambda t: (0, 0, 0, t, 0, 0)),
        ],
        out_shape=[
            jax.ShapeDtypeStruct((256, CH), BF16),
            jax.ShapeDtypeStruct((256, CH), BF16),
            jax.ShapeDtypeStruct((NY, NC, NX, TAPS, 64, LANES), BF16),
        ],
        scratch_shapes=[
            pltpu.VMEM((256, CH), F32),
            pltpu.VMEM((256, CH), F32),
            pltpu.VMEM((3, 320, CH), BF16),
        ],
        compiler_params=pltpu.CompilerParams(vmem_limit_bytes=32 << 20),
        cost_estimate=pl.CostEstimate(
            flops=3 * 2 * 256 * 4608 * 512, bytes_accessed=11 << 20, transcendentals=0
        ),
        name="conv_terms",
    )(xs, gs, ogt, kernel)


def start_spread(gram):
    size = gram.shape[0]
    i = lax.broadcasted_iota(jnp.int32, (size, size), 0)
    j = lax.broadcasted_iota(jnp.int32, (size, size), 1)
    eye = jnp.where(i == j, 1.0, 0.0)
    trace = jnp.sum(gram * eye, keepdims=True)
    spread = gram / (trace + 1e-06) - eye * (1.0 / size)
    return spread / (jnp.sqrt(jnp.sum(spread * spread, keepdims=True)) + 1e-06)


def combiners(grams, mix):
    spreads = [start_spread(gram) for gram in grams]
    for sweep in range(NS_STEPS - 1):
        rounded = [s.astype(BF16) for s in spreads]
        squares = [dot(r, r).astype(BF16) for r in rounded]
        spreads = [
            1.5 * s - 0.5 * dot(r, q) for s, r, q in zip(spreads, rounded, squares)
        ]
    parts = [split(s) for s in spreads]
    squares = [dot(high, high).astype(BF16) for high, low in parts]
    mixed = [dot(mix, high) + dot(mix, low) for high, low in parts]
    wide = mix.astype(F32)
    return [
        (0.5 * wide + 0.75 * m - 0.25 * dot(m.astype(BF16), q)).astype(BF16)
        for m, q in zip(mixed, squares)
    ]


def carried_gram(combiner, gram):
    high, low = split(gram)
    first = dot(combiner, high) + dot(combiner, low)
    high, low = split(first)
    return dot_t(high, combiner) + dot_t(low, combiner)


def tree_kernel(
    wt, bands, proj, mixers, gk, sketch,
    ro, rc, ry, w2, rx, wz, rz, m0, m1, ma, mb, da, db, po, pr, fr, gm, lsem, ssem, rsem,
):
    row, col = lax.axis_index("rows"), lax.axis_index("cols")
    z, x = lax.div(row, NX), lax.rem(row, NX)
    y, core = lax.div(col, NC), lax.rem(col, NC)

    def at(zz, xx, yy, cc):
        return (zz * NX + xx, yy * NC + cc)

    x_peers = [at(z, lax.rem(x + d, NX), y, core) for d in range(1, NX)]
    y_peers = [at(z, x, lax.rem(y + d, NY), core) for d in range(1, NY)]
    z_peers = [at(lax.rem(z + d, NZ), x, y, core) for d in range(1, NZ)]
    core_peer = at(z, x, y, 1 - core)

    barrier = pltpu.get_barrier_semaphore()
    peers = x_peers + y_peers + z_peers + [core_peer]
    for peer in peers:
        pl.semaphore_signal(barrier, inc=1, device_id=peer, device_id_type=MESH)

    started = []

    def send(src, dst, i, peer):
        copy = pltpu.make_async_remote_copy(
            src_ref=src,
            dst_ref=dst,
            send_sem=ssem.at[i],
            recv_sem=rsem.at[i],
            device_id=peer,
            device_id_type=MESH,
        )
        copy.start()
        started.append(copy)
        return copy

    own_terms = pltpu.make_async_copy(wt.at[:, core], ro, lsem.at[0])
    own_terms.start()
    pl.semaphore_wait(barrier, len(peers))
    core_copy = send(wt.at[:, 1 - core], rc, 0, core_peer)

    for j in range(NX):
        slot = lax.rem(j - x + NX, NX)
        p = proj[slot]
        for t in range(TAPS):
            a, b = t // 3, t % 3
            part = dot(p, bands[b, slot, a * 32 : a * 32 + 256, :]).astype(BF16)
            for i in range(4):
                q, lane = (4 * t + i) // 9, (4 * t + i) % 9
                m0[
                    j // 2, q, (j % 2) * RANK : (j % 2 + 1) * RANK,
                    lane * LANES : (lane + 1) * LANES,
                ] = part[:, i * LANES : (i + 1) * LANES]
    grams = []
    for pair in range(2):
        gram = dot_t(m0[pair, 0], m0[pair, 0])
        for q in range(1, 4):
            gram += dot_t(m0[pair, q], m0[pair, q])
        grams.append(gram)
    for pair, combiner in enumerate(combiners(grams, mixers[0])):
        for q in range(4):
            m1[q, pair * RANK : (pair + 1) * RANK, :] = dot(combiner, m0[pair, q]).astype(BF16)

    own_terms.wait()
    core_copy.wait_recv()

    @pl.loop(0, 36)
    def _(i):
        ro[:, i] = (ro[:, i].astype(F32) + rc[:, i].astype(F32)).astype(BF16)

    y_copies = [
        send(ro.at[lax.rem(y + d, NY)], ry.at[d - 1], d, y_peers[d - 1]) for d in range(1, NY)
    ]

    gram = dot_t(m1[0], m1[0])
    for q in range(1, 4):
        gram += dot_t(m1[q], m1[q])
    (combiner,) = combiners([gram], mixers[0])
    ma[0] = dot(combiner, m1[x]).astype(BF16)

    def y_stage():
        for copy in y_copies:
            copy.wait_recv()

        @pl.loop(0, 36)
        def _(i):
            total = ro[y, i].astype(F32)
            for d in range(NY - 1):
                total += ry[d, i].astype(F32)
            w2[i] = total.astype(BF16)

        return [
            send(w2.at[pl.ds(lax.rem(x + d, NX) * 9, 9)], rx.at[d - 1], 3 + d, x_peers[d - 1])
            for d in range(1, NX)
        ]

    def x_stage():
        for copy in x_copies:
            copy.wait_recv()
        for pair in range(5):
            halves = []
            for t in (2 * pair, 2 * pair + 1):
                if t < TAPS:
                    total = w2[x * 9 + t].astype(F32)
                    for d in range(NX - 1):
                        total += rx[d, t].astype(F32)
                else:
                    total = jnp.zeros((64, LANES), F32)
                halves.append(total)
            turned = jnp.concatenate(halves, axis=0).T.astype(BF16)
            for k in range(NZ):
                wz[k, pair] = turned[k * 16 : (k + 1) * 16, :]
        return [
            send(wz.at[lax.rem(z + d, NZ)], rz.at[d - 1], 6 + d, z_peers[d - 1])
            for d in range(1, NZ)
        ]

    def flip(value, bit):
        return value + bit - 2 * bit * lax.rem(lax.div(value, bit), 2)

    levels = [
        (at(flip(z, 1), x, y, core), lax.rem(z, 2), 0),
        (at(flip(z, 2), x, y, core), lax.rem(lax.div(z, 2), 2), 0),
        (at(flip(z, 4), x, y, core), lax.div(z, 4), 0),
        (core_peer, core, 1),
        (at(z, x, flip(y, 1), core), lax.rem(y, 2), 1),
        (at(z, x, flip(y, 2), core), lax.div(y, 2), 1),
    ]
    for level, (peer, upper, which) in enumerate(levels):
        base = 14 + 5 * level
        slice_copy = send(ma.at[level], mb.at[level], base, peer)
        da[level] = carried_gram(combiner, gram)
        gram_copy = send(da.at[level], db.at[level], base + 1, peer)
        if level == 1:
            x_copies = y_stage()
        if level == 2:
            z_copies = x_stage()
        mix = mixers[which]
        mix = jnp.where(
            upper == 0, mix, jnp.concatenate([mix[:, RANK:], mix[:, :RANK]], axis=1)
        )
        slice_copy.wait_recv()
        cross = dot_t(ma[level], mb[level]).astype(BF16)
        po[level] = cross
        cross_copies = [
            send(po.at[level], pr.at[level, d - 1], base + 1 + d, x_peers[d - 1])
            for d in range(1, NX)
        ]
        gram_copy.wait_recv()
        for copy in cross_copies:
            copy.wait_recv()
        cross = cross.astype(F32)
        for d in range(NX - 1):
            cross += pr[level, d].astype(F32)
        gm[0:RANK, 0:RANK] = da[level]
        gm[0:RANK, RANK:] = cross
        gm[RANK:, 0:RANK] = cross.T
        gm[RANK:, RANK:] = db[level]
        gram = gm[...]
        (combiner,) = combiners([gram], mix)
        stacked = jnp.concatenate([ma[level], mb[level]], axis=0)
        ma[level + 1] = dot(combiner, stacked).astype(BF16)

    last = len(levels)
    own_rows = pl.ds(pl.multiple_of(col * 16, 16), 16)
    fr[0] = ma[last, own_rows, :]
    final_copies = [
        send(ma.at[last, own_rows], fr.at[d], 43 + d, x_peers[d - 1]) for d in range(1, NX)
    ]
    for copy in z_copies:
        copy.wait_recv()
    for pair in range(5):
        total = wz[z, pair].astype(F32)
        for d in range(NZ - 1):
            total += rz[d, pair].astype(F32)
        gk[2 * pair] = total[:, :64]
        if 2 * pair + 1 < TAPS:
            gk[2 * pair + 1] = total[:, 64:]
    for copy in final_copies:
        copy.wait_recv()
    k = lax.broadcasted_iota(jnp.int32, (QUART, 144), 0)
    j = lax.broadcasted_iota(jnp.int32, (QUART, 144), 1)
    chosen = jnp.where(k == j + lax.rem(row, 8) * 144, 1.0, 0.0).astype(BF16)
    held = fr[lax.rem(x - lax.div(z, 2) + NX, NX)]
    sketch[...] = dot(held, chosen).astype(BF16)
    for copy in started:
        copy.wait_send()


def tree_call(wt, bands, proj, mixers):
    vmem = pl.BlockSpec(memory_space=pltpu.VMEM)
    return pl.pallas_call(
        tree_kernel,
        in_specs=[pl.BlockSpec(memory_space=pl.ANY), vmem, vmem, vmem],
        out_specs=[vmem, vmem],
        out_shape=[
            jax.ShapeDtypeStruct((TAPS, 16, 64), F32),
            jax.ShapeDtypeStruct((16, 144), BF16),
        ],
        scratch_shapes=[
            pltpu.VMEM((NY, 36, 64, LANES), BF16),
            pltpu.VMEM((NY, 36, 64, LANES), BF16),
            pltpu.VMEM((NY - 1, 36, 64, LANES), BF16),
            pltpu.VMEM((36, 64, LANES), BF16),
            pltpu.VMEM((NX - 1, 9, 64, LANES), BF16),
            pltpu.VMEM((NZ, 5, 16, LANES), BF16),
            pltpu.VMEM((NZ - 1, 5, 16, LANES), BF16),
            pltpu.VMEM((2, 4, 2 * RANK, QUART), BF16),
            pltpu.VMEM((4, 2 * RANK, QUART), BF16),
            pltpu.VMEM((7, RANK, QUART), BF16),
            pltpu.VMEM((6, RANK, QUART), BF16),
            pltpu.VMEM((6, RANK, RANK), F32),
            pltpu.VMEM((6, RANK, RANK), F32),
            pltpu.VMEM((6, RANK, RANK), BF16),
            pltpu.VMEM((6, 3, RANK, RANK), BF16),
            pltpu.VMEM((4, 16, QUART), BF16),
            pltpu.VMEM((2 * RANK, 2 * RANK), F32),
            pltpu.SemaphoreType.DMA((1,)),
            pltpu.SemaphoreType.DMA((47,)),
            pltpu.SemaphoreType.DMA((47,)),
        ],
        compiler_params=pltpu.CompilerParams(
            collective_id=0, has_side_effects=True, vmem_limit_bytes=48 << 20
        ),
        name="merge_tree",
    )(wt, bands, proj, mixers)


def padded_2(x, sides, width):
    for axis, dim in sides:
        size, length = (lax.axis_size(axis), x.shape[dim])
        up = [(i, (i + 1) % size) for i in range(size - 1)]
        down = [(j, i) for i, j in up]
        last = lax.slice_in_dim(x, length - width, length, axis=dim)
        first = lax.slice_in_dim(x, 0, width, axis=dim)
        before = lax.ppermute(last, axis, up)
        after = lax.ppermute(first, axis, down)
        x = jnp.concatenate([before, x, after], axis=dim)
    return x


def shifted(padded):
    lead = padded.shape[:-3]
    rows, channels = padded.shape[-3], padded.shape[-1]
    return jnp.stack(
        [
            lax.slice_in_dim(padded, b, b + 32, axis=padded.ndim - 2).reshape(
                lead + (rows * 32, channels)
            )
            for b in range(3)
        ]
    )


def ring_gather(v):
    pieces = [v]
    for d in range(1, NX):
        moves = [(z * NX + (x + d) % NX, z * NX + x) for z in range(NZ) for x in range(NX)]
        pieces.append(lax.ppermute(v, "rows", moves))
    return jnp.stack(pieces)


def body(features, kernel, out_grad, projector, mixers):
    band_rows, band_cols, channels = features.shape
    pixels = band_rows * band_cols
    projectors = ring_gather(projector)
    padded = padded_2(features, (("rows", 0), ("cols", 1)), 1)
    grad_padded = padded_2(out_grad, (("rows", 0), ("cols", 1)), 1)
    bands = shifted(ring_gather(padded))
    output, grad_features, terms = local_call(
        shifted(padded),
        shifted(grad_padded),
        out_grad.reshape(pixels, channels).T,
        kernel.reshape(TAPS, channels, channels),
    )
    terms = terms.reshape(NY, NC, NX * TAPS, 64, LANES)
    grad_kernel, own_block = tree_call(terms, bands, projectors, mixers)
    shape = (band_rows, band_cols, channels)
    return (output.reshape(shape), grad_features.reshape(shape), grad_kernel, own_block)


def solution(mesh):
    in_specs = (P("rows", "cols", None), P(), P("rows", "cols", None), P("rows", "cols"), P())
    out_specs = (
        P("rows", "cols", None),
        P("rows", "cols", None),
        P(None, "rows", "cols"),
        P("cols", "rows"),
    )
    return jax.shard_map(body, mesh=mesh, in_specs=in_specs, out_specs=out_specs, check_vma=False)
```

```python
import jax
import jax.numpy as jnp
from jax import lax
from jax.experimental import pallas as pl
from jax.experimental.pallas import tpu as pltpu
from jax.sharding import PartitionSpec as P

NS_STEPS = 5
NX, NZ, NY, NC = 4, 8, 4, 2
LANES = 128
CH = 512
RANK = 128
TAPS = 9
QUART = 1152
MESH = pl.DeviceIdType.MESH
F32 = jnp.float32
BF16 = jnp.bfloat16


def dot(a, b):
    return jnp.dot(a, b, preferred_element_type=F32)


def dot_t(a, b):
    return lax.dot_general(a, b, (((1,), (1,)), ((), ())), preferred_element_type=F32)


def split(v):
    high = v.astype(BF16)
    return high, (v - high.astype(F32)).astype(BF16)


def start_spread(gram):
    size = gram.shape[0]
    i = lax.broadcasted_iota(jnp.int32, (size, size), 0)
    j = lax.broadcasted_iota(jnp.int32, (size, size), 1)
    eye = jnp.where(i == j, 1.0, 0.0)
    trace = jnp.sum(gram * eye, keepdims=True)
    spread = gram / (trace + 1e-06) - eye * (1.0 / size)
    return spread / (jnp.sqrt(jnp.sum(spread * spread, keepdims=True)) + 1e-06)


def combiners(grams, mix):
    spreads = [start_spread(gram) for gram in grams]
    for sweep in range(NS_STEPS - 1):
        rounded = [s.astype(BF16) for s in spreads]
        squares = [dot(r, r).astype(BF16) for r in rounded]
        spreads = [
            1.5 * s - 0.5 * dot(r, q) for s, r, q in zip(spreads, rounded, squares)
        ]
    parts = [split(s) for s in spreads]
    squares = [dot(high, high).astype(BF16) for high, low in parts]
    mixed = [dot(mix, high) + dot(mix, low) for high, low in parts]
    wide = mix.astype(F32)
    return [
        (0.5 * wide + 0.75 * m - 0.25 * dot(m.astype(BF16), q)).astype(BF16)
        for m, q in zip(mixed, squares)
    ]


def carried_gram(combiner, gram):
    high, low = split(gram)
    first = dot(combiner, high) + dot(combiner, low)
    high, low = split(first)
    return dot_t(high, combiner) + dot_t(low, combiner)


def shift_columns(held, edges, slot_at):
    row_in = lax.broadcasted_iota(jnp.int32, (32, CH), 0)
    left, right = edges
    for h in range(10):
        rows = slice(h * 32, h * 32 + 32)
        mid = held[slot_at + (1, rows)].astype(F32)
        before = jnp.where(row_in == 0, left[h : h + 1], pltpu.roll(mid, 1, 0))
        after = jnp.where(row_in == 31, right[h : h + 1], pltpu.roll(mid, 31, 0))
        held[slot_at + (0, rows)] = before.astype(BF16)
        held[slot_at + (2, rows)] = after.astype(BF16)


def step_kernel(
    feat, grad, strips, kern, proj, mixers, out, gfeat, gk, sketch,
    bx, be, pj, gs, edge, line, xsp, ogt, kv, wt, acc,
    ro, rc, ry, w2, rx, wz, rz, m0, m1, ma, mb, da, db, po, pr, fr, gm, lsem, ssem, rsem,
):
    row, col = lax.axis_index("rows"), lax.axis_index("cols")
    n_rows, n_cols = NX * NZ, NY * NC
    z, x = lax.div(row, NX), lax.rem(row, NX)
    y, core = lax.div(col, NC), lax.rem(col, NC)

    def at(zz, xx, yy, cc):
        return (zz * NX + xx, yy * NC + cc)

    x_peers = [at(z, lax.rem(x + d, NX), y, core) for d in range(1, NX)]
    y_peers = [at(z, x, lax.rem(y + d, NY), core) for d in range(1, NY)]
    z_peers = [at(lax.rem(z + d, NZ), x, y, core) for d in range(1, NZ)]
    core_peer = at(z, x, y, 1 - core)
    above, below = lax.rem(row + n_rows - 1, n_rows), lax.rem(row + 1, n_rows)
    before, after = lax.rem(col + n_cols - 1, n_cols), lax.rem(col + 1, n_cols)
    around = [(r, c) for c in (before, after) for r in (above, row, below)]
    around += [(above, col), (below, col)]

    def fetch(src, dst, i):
        copy = pltpu.make_async_copy(src, dst, lsem.at[i])
        copy.start()
        return copy

    own_band = fetch(feat, bx.at[0, 1, 32:288], 0)
    own_grad = fetch(grad, gs.at[1, 32:288], 1)
    own_proj = fetch(proj, pj.at[0], 2)
    weights = fetch(kern, kv, 3)

    barrier = pltpu.get_barrier_semaphore()
    peers = x_peers + y_peers + z_peers + [core_peer] + around
    for peer in peers:
        pl.semaphore_signal(barrier, inc=1, device_id=peer, device_id_type=MESH)
    pl.semaphore_wait(barrier, len(peers))

    started = []

    def send(src, dst, i, peer):
        copy = pltpu.make_async_remote_copy(
            src_ref=src,
            dst_ref=dst,
            send_sem=ssem.at[i],
            recv_sem=rsem.at[i],
            device_id=peer,
            device_id_type=MESH,
        )
        copy.start()
        started.append(copy)
        return copy

    halo = []
    for k, r in enumerate((below, row, above)):
        halo.append(send(strips.at[0], edge.at[1, k], 47 + k, (r, before)))
        halo.append(send(strips.at[1], edge.at[0, k], 50 + k, (r, after)))
    halo.append(send(feat.at[224:256], bx.at[0, 1, 0:32], 53, (below, col)))
    halo.append(send(feat.at[0:32], bx.at[0, 1, 288:320], 54, (above, col)))
    halo.append(send(grad.at[224:256], gs.at[1, 0:32], 55, (below, col)))
    halo.append(send(grad.at[0:32], gs.at[1, 288:320], 56, (above, col)))
    main = [
        (
            send(feat, bx.at[d, 1, 32:288], 56 + d, x_peers[d - 1]),
            send(proj, pj.at[d], 59 + d, x_peers[d - 1]),
        )
        for d in range(1, NX)
    ]
    for copy in (own_band, own_grad, own_proj):
        copy.wait()
    ogt[...] = gs[1, 32:288].astype(F32).T.astype(BF16)
    for copy in halo:
        copy.wait_recv()

    def kept(value, outside):
        return jnp.where(outside, jnp.zeros_like(value), value)

    top, bottom = row == 0, row == n_rows - 1
    for held in (bx.at[0, 1], gs.at[1]):
        held[0:32] = kept(held[0:32], top)
        held[288:320] = kept(held[288:320], bottom)
    line[...] = jnp.zeros_like(line)
    for side, outside in enumerate((col == 0, col == n_cols - 1)):
        up, mid, down = [kept(edge[side, k].astype(F32), outside) for k in range(3)]
        for which in range(2):
            rows = 8 * which
            line[which, side, 0:1] = kept(up[rows + 7 : rows + 8], top)
            line[which, side, 1:9] = mid[rows : rows + 8]
            line[which, side, 9:10] = kept(down[rows : rows + 1], bottom)
    be[0] = line[0].astype(BF16)
    ends = [
        (
            send(bx.at[0, 1, 0:32], bx.at[d, 1, 0:32], 62 + d, x_peers[d - 1]),
            send(bx.at[0, 1, 288:320], bx.at[d, 1, 288:320], 65 + d, x_peers[d - 1]),
            send(be.at[0], be.at[d], 68 + d, x_peers[d - 1]),
        )
        for d in range(1, NX)
    ]
    shift_columns(bx, (line[0, 0], line[0, 1]), (0,))

    ci = lax.broadcasted_iota(jnp.int32, (CH, CH), 0)
    to = lax.broadcasted_iota(jnp.int32, (CH, CH), 1)
    source = lax.rem(lax.div(to, 16), NZ) * 64 + lax.div(to, LANES) * 16 + lax.rem(to, 16)
    perm = jnp.where(ci == source, 1.0, 0.0).astype(BF16)
    for b in range(3):
        xsp[b] = dot(bx[0, b], perm).astype(BF16)

    @pl.loop(0, TAPS)
    def _(t):
        start = pl.multiple_of(lax.div(t, 3) * 32, 32)
        terms = dot(ogt[...], xsp[lax.rem(t, 3), pl.ds(start, 256), :]).astype(BF16)
        for yy in range(NY):
            for cc in range(NC):
                first = (yy * NC + cc) * 64
                for xx in range(NX):
                    wt[yy, cc, xx * TAPS + t] = terms[
                        first : first + 64, xx * LANES : (xx + 1) * LANES
                    ]

    core_copy = send(wt.at[:, 1 - core], rc, 0, core_peer)
    shift_columns(gs, (line[1, 0], line[1, 1]), ())

    for d in range(1, NX):
        for copy in main[d - 1] + ends[d - 1]:
            copy.wait_recv()
        edges = be[d].astype(F32)
        shift_columns(bx, (edges[0], edges[1]), (d,))

    for j in range(NX):
        slot = lax.rem(x - j + NX, NX)
        p = pj[slot]
        for t in range(TAPS):
            a, b = t // 3, t % 3
            part = dot(p, bx[slot, b, a * 32 : a * 32 + 256, :]).astype(BF16)
            for i in range(4):
                q, lane = (4 * t + i) // 9, (4 * t + i) % 9
                m0[
                    j // 2, q, (j % 2) * RANK : (j % 2 + 1) * RANK,
                    lane * LANES : (lane + 1) * LANES,
                ] = part[:, i * LANES : (i + 1) * LANES]
    grams = []
    for pair in range(2):
        gram = dot_t(m0[pair, 0], m0[pair, 0])
        for q in range(1, 4):
            gram += dot_t(m0[pair, q], m0[pair, q])
        grams.append(gram)
    for pair, combiner in enumerate(combiners(grams, mixers[0])):
        for q in range(4):
            m1[q, pair * RANK : (pair + 1) * RANK, :] = dot(combiner, m0[pair, q]).astype(BF16)

    gram = dot_t(m1[0], m1[0])
    for q in range(1, 4):
        gram += dot_t(m1[q], m1[q])
    (combiner,) = combiners([gram], mixers[0])
    ma[0] = dot(combiner, m1[x]).astype(BF16)

    def core_stage():
        core_copy.wait_recv()

        @pl.loop(0, 36)
        def _(i):
            ro[:, i] = (wt[:, core, i].astype(F32) + rc[:, i].astype(F32)).astype(BF16)

        return [
            send(ro.at[lax.rem(y + d, NY)], ry.at[d - 1], d, y_peers[d - 1])
            for d in range(1, NY)
        ]

    def forward():
        weights.wait()
        acc[...] = jnp.zeros_like(acc)

        @pl.loop(0, TAPS)
        def _(t):
            start = pl.multiple_of(lax.div(t, 3) * 32, 32)
            acc[...] += dot(bx[0, lax.rem(t, 3), pl.ds(start, 256), :], kv[t])

        out[...] = acc[...].astype(BF16)

    def backward():
        acc[...] = jnp.zeros_like(acc)

        @pl.loop(0, TAPS)
        def _(t):
            start = pl.multiple_of((2 - lax.div(t, 3)) * 32, 32)
            acc[...] += dot_t(gs[2 - lax.rem(t, 3), pl.ds(start, 256), :], kv[t])

        gfeat[...] = acc[...].astype(BF16)

    def y_stage():
        for copy in y_copies:
            copy.wait_recv()

        @pl.loop(0, 36)
        def _(i):
            total = ro[y, i].astype(F32)
            for d in range(NY - 1):
                total += ry[d, i].astype(F32)
            w2[i] = total.astype(BF16)

        return [
            send(w2.at[pl.ds(lax.rem(x + d, NX) * 9, 9)], rx.at[d - 1], 3 + d, x_peers[d - 1])
            for d in range(1, NX)
        ]

    def x_stage():
        for copy in x_copies:
            copy.wait_recv()
        for pair in range(5):
            halves = []
            for t in (2 * pair, 2 * pair + 1):
                if t < TAPS:
                    total = w2[x * 9 + t].astype(F32)
                    for d in range(NX - 1):
                        total += rx[d, t].astype(F32)
                else:
                    total = jnp.zeros((64, LANES), F32)
                halves.append(total)
            turned = jnp.concatenate(halves, axis=0).T.astype(BF16)
            for k in range(NZ):
                wz[k, pair] = turned[k * 16 : (k + 1) * 16, :]
        return [
            send(wz.at[lax.rem(z + d, NZ)], rz.at[d - 1], 6 + d, z_peers[d - 1])
            for d in range(1, NZ)
        ]

    def flip(value, bit):
        return value + bit - 2 * bit * lax.rem(lax.div(value, bit), 2)

    levels = [
        (at(flip(z, 1), x, y, core), lax.rem(z, 2), 0),
        (at(flip(z, 2), x, y, core), lax.rem(lax.div(z, 2), 2), 0),
        (at(flip(z, 4), x, y, core), lax.div(z, 4), 0),
        (core_peer, core, 1),
        (at(z, x, flip(y, 1), core), lax.rem(y, 2), 1),
        (at(z, x, flip(y, 2), core), lax.div(y, 2), 1),
    ]
    for level, (peer, upper, which) in enumerate(levels):
        base = 14 + 5 * level
        slice_copy = send(ma.at[level], mb.at[level], base, peer)
        da[level] = carried_gram(combiner, gram)
        gram_copy = send(da.at[level], db.at[level], base + 1, peer)
        if level == 0:
            y_copies = core_stage()
            forward()
        if level == 1:
            backward()
        if level == 2:
            x_copies = y_stage()
        if level == 4:
            z_copies = x_stage()
        mix = mixers[which]
        mix = jnp.where(
            upper == 0, mix, jnp.concatenate([mix[:, RANK:], mix[:, :RANK]], axis=1)
        )
        slice_copy.wait_recv()
        cross = dot_t(ma[level], mb[level]).astype(BF16)
        po[level] = cross
        cross_copies = [
            send(po.at[level], pr.at[level, d - 1], base + 1 + d, x_peers[d - 1])
            for d in range(1, NX)
        ]
        gram_copy.wait_recv()
        for copy in cross_copies:
            copy.wait_recv()
        cross = cross.astype(F32)
        for d in range(NX - 1):
            cross += pr[level, d].astype(F32)
        gm[0:RANK, 0:RANK] = da[level]
        gm[0:RANK, RANK:] = cross
        gm[RANK:, 0:RANK] = cross.T
        gm[RANK:, RANK:] = db[level]
        gram = gm[...]
        (combiner,) = combiners([gram], mix)
        stacked = jnp.concatenate([ma[level], mb[level]], axis=0)
        ma[level + 1] = dot(combiner, stacked).astype(BF16)

    last = len(levels)
    own_rows = pl.ds(pl.multiple_of(col * 16, 16), 16)
    fr[0] = ma[last, own_rows, :]
    final_copies = [
        send(ma.at[last, own_rows], fr.at[d], 43 + d, x_peers[d - 1]) for d in range(1, NX)
    ]
    for copy in z_copies:
        copy.wait_recv()
    for pair in range(5):
        total = wz[z, pair].astype(F32)
        for d in range(NZ - 1):
            total += rz[d, pair].astype(F32)
        gk[2 * pair] = total[:, :64]
        if 2 * pair + 1 < TAPS:
            gk[2 * pair + 1] = total[:, 64:]
    for copy in final_copies:
        copy.wait_recv()
    k = lax.broadcasted_iota(jnp.int32, (QUART, 144), 0)
    j = lax.broadcasted_iota(jnp.int32, (QUART, 144), 1)
    chosen = jnp.where(k == j + lax.rem(row, 8) * 144, 1.0, 0.0).astype(BF16)
    held = fr[lax.rem(x - lax.div(z, 2) + NX, NX)]
    sketch[...] = dot(held, chosen).astype(BF16)
    for copy in started:
        copy.wait_send()


def step_call(feat, grad, strips, kern, proj, mixers):
    vmem = pl.BlockSpec(memory_space=pltpu.VMEM)
    return pl.pallas_call(
        step_kernel,
        in_specs=[pl.BlockSpec(memory_space=pl.ANY)] * 5 + [vmem],
        out_specs=[vmem] * 4,
        out_shape=[
            jax.ShapeDtypeStruct((256, CH), BF16),
            jax.ShapeDtypeStruct((256, CH), BF16),
            jax.ShapeDtypeStruct((TAPS, 16, 64), F32),
            jax.ShapeDtypeStruct((16, 144), BF16),
        ],
        scratch_shapes=[
            pltpu.VMEM((NX, 3, 320, CH), BF16),
            pltpu.VMEM((NX, 2, 16, CH), BF16),
            pltpu.VMEM((NX, RANK, 256), BF16),
            pltpu.VMEM((3, 320, CH), BF16),
            pltpu.VMEM((2, 3, 16, CH), BF16),
            pltpu.VMEM((2, 2, 16, CH), F32),
            pltpu.VMEM((3, 320, CH), BF16),
            pltpu.VMEM((CH, 256), BF16),
            pltpu.VMEM((TAPS, CH, CH), BF16),
            pltpu.VMEM((NY, NC, 36, 64, LANES), BF16),
            pltpu.VMEM((256, CH), F32),
            pltpu.VMEM((NY, 36, 64, LANES), BF16),
            pltpu.VMEM((NY, 36, 64, LANES), BF16),
            pltpu.VMEM((NY - 1, 36, 64, LANES), BF16),
            pltpu.VMEM((36, 64, LANES), BF16),
            pltpu.VMEM((NX - 1, 9, 64, LANES), BF16),
            pltpu.VMEM((NZ, 5, 16, LANES), BF16),
            pltpu.VMEM((NZ - 1, 5, 16, LANES), BF16),
            pltpu.VMEM((2, 4, 2 * RANK, QUART), BF16),
            pltpu.VMEM((4, 2 * RANK, QUART), BF16),
            pltpu.VMEM((7, RANK, QUART), BF16),
            pltpu.VMEM((6, RANK, QUART), BF16),
            pltpu.VMEM((6, RANK, RANK), F32),
            pltpu.VMEM((6, RANK, RANK), F32),
            pltpu.VMEM((6, RANK, RANK), BF16),
            pltpu.VMEM((6, 3, RANK, RANK), BF16),
            pltpu.VMEM((4, 16, QUART), BF16),
            pltpu.VMEM((2 * RANK, 2 * RANK), F32),
            pltpu.SemaphoreType.DMA((4,)),
            pltpu.SemaphoreType.DMA((72,)),
            pltpu.SemaphoreType.DMA((72,)),
        ],
        compiler_params=pltpu.CompilerParams(
            collective_id=0, has_side_effects=True, vmem_limit_bytes=56 << 20
        ),
        name="conv_step",
    )(feat, grad, strips, kern, proj, mixers)


def body(features, kernel, out_grad, projector, mixers):
    shape = features.shape
    channels = shape[2]
    strips = jnp.stack(
        [
            jnp.concatenate([features[:, w], out_grad[:, w]], axis=0)
            for w in (0, shape[1] - 1)
        ]
    )
    output, grad_features, grad_kernel, own_block = step_call(
        features.reshape(-1, channels),
        out_grad.reshape(-1, channels),
        strips,
        kernel.reshape(TAPS, channels, channels),
        projector,
        mixers,
    )
    return (output.reshape(shape), grad_features.reshape(shape), grad_kernel, own_block)


def solution(mesh):
    in_specs = (P("rows", "cols", None), P(), P("rows", "cols", None), P("rows", "cols"), P())
    out_specs = (
        P("rows", "cols", None),
        P("rows", "cols", None),
        P(None, "rows", "cols"),
        P("cols", "rows"),
    )
    return jax.shard_map(body, mesh=mesh, in_specs=in_specs, out_specs=out_specs, check_vma=False)
```

```python
import jax
import jax.numpy as jnp
from jax import lax
from jax.experimental import pallas as pl
from jax.experimental.pallas import tpu as pltpu
from jax.sharding import PartitionSpec as P

NS_STEPS = 5
NX, NZ, NY, NC = 4, 8, 4, 2
LANES = 128
CH = 512
RANK = 128
TAPS = 9
QUART = 1152
HALF = 640
MESH = pl.DeviceIdType.MESH
F32 = jnp.float32
BF16 = jnp.bfloat16


def dot(a, b):
    return jnp.dot(a, b, preferred_element_type=F32)


def dot_t(a, b):
    return lax.dot_general(a, b, (((1,), (1,)), ((), ())), preferred_element_type=F32)


def split(v):
    high = v.astype(BF16)
    return high, (v - high.astype(F32)).astype(BF16)


def start_spread(gram):
    size = gram.shape[0]
    i = lax.broadcasted_iota(jnp.int32, (size, size), 0)
    j = lax.broadcasted_iota(jnp.int32, (size, size), 1)
    eye = jnp.where(i == j, 1.0, 0.0)
    trace = jnp.sum(gram * eye, keepdims=True)
    spread = gram / (trace + 1e-06) - eye * (1.0 / size)
    return spread / (jnp.sqrt(jnp.sum(spread * spread, keepdims=True)) + 1e-06)


def combiners(grams, mix):
    spreads = [start_spread(gram) for gram in grams]
    for sweep in range(NS_STEPS - 1):
        rounded = [s.astype(BF16) for s in spreads]
        squares = [dot(r, r).astype(BF16) for r in rounded]
        spreads = [
            1.5 * s - 0.5 * dot(r, q) for s, r, q in zip(spreads, rounded, squares)
        ]
    parts = [split(s) for s in spreads]
    squares = [dot(high, high).astype(BF16) for high, low in parts]
    mixed = [dot(mix, high) + dot(mix, low) for high, low in parts]
    wide = mix.astype(F32)
    return [
        (0.5 * wide + 0.75 * m - 0.25 * dot(m.astype(BF16), q)).astype(BF16)
        for m, q in zip(mixed, squares)
    ]


def carried_gram(combiner, gram):
    high, low = split(gram)
    first = dot(combiner, high) + dot(combiner, low)
    high, low = split(first)
    return dot_t(high, combiner) + dot_t(low, combiner)


def shift_columns(held, edges, slot_at):
    row_in = lax.broadcasted_iota(jnp.int32, (32, CH), 0)
    left, right = edges
    for h in range(10):
        rows = slice(h * 32, h * 32 + 32)
        mid = held[slot_at + (1, rows)].astype(F32)
        before = jnp.where(row_in == 0, left[h : h + 1], pltpu.roll(mid, 1, 0))
        after = jnp.where(row_in == 31, right[h : h + 1], pltpu.roll(mid, 31, 0))
        held[slot_at + (0, rows)] = before.astype(BF16)
        held[slot_at + (2, rows)] = after.astype(BF16)


def step_kernel(
    feat, grad, kern, proj, mixers, out, gfeat, gk, sketch,
    bx, be, pj, gs, strips, cut, edge, line, xsp, ogt, kv, wt, acc,
    ro, rc, ry, w2, rx, wz, rz, m0, m1, mo, ma, mb, da, db, va, vb, po, pr, fr, gm, lsem, ssem, rsem,
):
    row, col = lax.axis_index("rows"), lax.axis_index("cols")
    n_rows, n_cols = NX * NZ, NY * NC
    z, x = lax.div(row, NX), lax.rem(row, NX)
    y, core = lax.div(col, NC), lax.rem(col, NC)

    def at(zz, xx, yy, cc):
        return (zz * NX + xx, yy * NC + cc)

    x_peers = [at(z, lax.rem(x + d, NX), y, core) for d in range(1, NX)]
    y_peers = [at(z, x, lax.rem(y + d, NY), core) for d in range(1, NY)]
    z_peers = [at(lax.rem(z + d, NZ), x, y, core) for d in range(1, NZ)]
    core_peer = at(z, x, y, 1 - core)
    half = lax.rem(z, 2)
    mate = z + 1 - 2 * half
    sum_peers = x_peers + [at(mate, lax.rem(x + d, NX), y, core) for d in range(NX)]
    above, below = lax.rem(row + n_rows - 1, n_rows), lax.rem(row + 1, n_rows)
    before, after = lax.rem(col + n_cols - 1, n_cols), lax.rem(col + 1, n_cols)
    around = [(r, c) for c in (before, after) for r in (above, row, below)]
    around += [(above, col), (below, col)]

    def fetch(src, dst, i):
        copy = pltpu.make_async_copy(src, dst, lsem.at[i])
        copy.start()
        return copy

    own_band = fetch(feat, bx.at[0, 1, 32:288], 0)
    own_grad = fetch(grad, gs.at[1, 32:288], 1)
    own_proj = fetch(proj, pj.at[0], 2)
    weights = fetch(kern, kv, 3)

    barrier = pltpu.get_barrier_semaphore()
    peers = sum_peers + y_peers + z_peers + [core_peer] + around
    for peer in peers:
        pl.semaphore_signal(barrier, inc=1, device_id=peer, device_id_type=MESH)
    own_band.wait()
    own_grad.wait()
    for which, held in enumerate((bx.at[0, 1], gs.at[1])):
        for h in range(8):
            at_row = 8 * which + h
            first = held[32 + h * 32 : 48 + h * 32].astype(F32)
            last = held[48 + h * 32 : 64 + h * 32].astype(F32)
            cut[0, at_row : at_row + 1] = first[0:1]
            cut[1, at_row : at_row + 1] = last[15:16]
    strips[...] = cut[...].astype(BF16)
    pl.semaphore_wait(barrier, len(peers))

    started = []

    def send(src, dst, i, peer):
        copy = pltpu.make_async_remote_copy(
            src_ref=src,
            dst_ref=dst,
            send_sem=ssem.at[i],
            recv_sem=rsem.at[i],
            device_id=peer,
            device_id_type=MESH,
        )
        copy.start()
        started.append(copy)
        return copy

    halo = []
    for k, r in enumerate((below, row, above)):
        halo.append(send(strips.at[0], edge.at[1, k], 77 + k, (r, before)))
        halo.append(send(strips.at[1], edge.at[0, k], 80 + k, (r, after)))
    halo.append(send(feat.at[224:256], bx.at[0, 1, 0:32], 83, (below, col)))
    halo.append(send(feat.at[0:32], bx.at[0, 1, 288:320], 84, (above, col)))
    halo.append(send(grad.at[224:256], gs.at[1, 0:32], 85, (below, col)))
    halo.append(send(grad.at[0:32], gs.at[1, 288:320], 86, (above, col)))
    main = {
        d: (
            send(feat, bx.at[d, 1, 32:288], 86 + d, x_peers[d - 1]),
            send(proj, pj.at[d], 89 + d, x_peers[d - 1]),
        )
        for d in (2, 1, 3)
    }
    own_proj.wait()
    ogt[...] = gs[1, 32:288].astype(F32).T.astype(BF16)
    for copy in halo:
        copy.wait_recv()

    def kept(value, outside):
        return jnp.where(outside, jnp.zeros_like(value), value)

    top, bottom = row == 0, row == n_rows - 1
    for held in (bx.at[0, 1], gs.at[1]):
        held[0:32] = kept(held[0:32], top)
        held[288:320] = kept(held[288:320], bottom)
    line[...] = jnp.zeros_like(line)
    for side, outside in enumerate((col == 0, col == n_cols - 1)):
        up, mid, down = [kept(edge[side, k].astype(F32), outside) for k in range(3)]
        for which in range(2):
            rows = 8 * which
            line[which, side, 0:1] = kept(up[rows + 7 : rows + 8], top)
            line[which, side, 1:9] = mid[rows : rows + 8]
            line[which, side, 9:10] = kept(down[rows : rows + 1], bottom)
    be[0] = line[0].astype(BF16)
    ends = {
        d: (
            send(bx.at[0, 1, 0:32], bx.at[d, 1, 0:32], 92 + d, x_peers[d - 1]),
            send(bx.at[0, 1, 288:320], bx.at[d, 1, 288:320], 95 + d, x_peers[d - 1]),
            send(be.at[0], be.at[d], 98 + d, x_peers[d - 1]),
        )
        for d in (2, 1, 3)
    }
    shift_columns(bx, (line[0, 0], line[0, 1]), (0,))

    ci = lax.broadcasted_iota(jnp.int32, (CH, CH), 0)
    to = lax.broadcasted_iota(jnp.int32, (CH, CH), 1)
    source = lax.rem(lax.div(to, 16), NZ) * 64 + lax.div(to, LANES) * 16 + lax.rem(to, 16)
    perm = jnp.where(ci == source, 1.0, 0.0).astype(BF16)
    for b in range(3):
        xsp[b] = dot(bx[0, b], perm).astype(BF16)

    @pl.loop(0, TAPS)
    def _(t):
        start = pl.multiple_of(lax.div(t, 3) * 32, 32)
        terms = dot(ogt[...], xsp[lax.rem(t, 3), pl.ds(start, 256), :]).astype(BF16)
        for yy in range(NY):
            for cc in range(NC):
                first = (yy * NC + cc) * 64
                for xx in range(NX):
                    wt[yy, cc, xx * TAPS + t] = terms[
                        first : first + 64, xx * LANES : (xx + 1) * LANES
                    ]

    core_copy = send(wt.at[:, 1 - core], rc, 0, core_peer)
    shift_columns(gs, (line[1, 0], line[1, 1]), ())

    def sketch_band(slot):
        j = lax.rem(x - slot + NX, NX)
        p = pj[slot]
        for t in range(TAPS):
            a, b = t // 3, t % 3
            part = dot(p, bx[slot, b, a * 32 : a * 32 + 256, :]).astype(BF16)
            for i in range(4):
                q, lane = (4 * t + i) // 9, (4 * t + i) % 9
                m0[j, q, :, lane * LANES : (lane + 1) * LANES] = part[
                    :, i * LANES : (i + 1) * LANES
                ]

    sketch_band(0)
    for d in (3, 1, 2):
        for copy in main[d] + ends[d]:
            copy.wait_recv()
        edges = be[d].astype(F32)
        shift_columns(bx, (edges[0], edges[1]), (d,))
        sketch_band(d)

    def pair_rows(pair, q):
        return jnp.concatenate([m0[2 * pair, q], m0[2 * pair + 1, q]], axis=0)

    grams = []
    for pair in range(2):
        gram = jnp.zeros((2 * RANK, 2 * RANK), F32)
        for q in range(4):
            stacked = pair_rows(pair, q)
            gram += dot_t(stacked, stacked)
        grams.append(gram)
    for pair, combiner in enumerate(combiners(grams, mixers[0])):
        for q in range(4):
            m1[q, pair * RANK : (pair + 1) * RANK, :] = dot(combiner, pair_rows(pair, q)).astype(
                BF16
            )

    gram = dot_t(m1[0], m1[0])
    for q in range(1, 4):
        gram += dot_t(m1[q], m1[q])
    (combiner,) = combiners([gram], mixers[0])
    merged = dot(combiner, m1[x])
    low, high = merged[:, :HALF], merged[:, QUART - HALF :]
    ma[0] = jnp.where(half == 0, low, high).astype(BF16)
    mo[...] = jnp.where(half == 0, high, low).astype(BF16)
    eye = lax.broadcasted_iota(jnp.int32, (RANK, RANK), 0) == lax.broadcasted_iota(
        jnp.int32, (RANK, RANK), 1
    )

    def core_stage():
        core_copy.wait_recv()

        @pl.loop(0, 36)
        def _(i):
            ro[:, i] = (wt[:, core, i].astype(F32) + rc[:, i].astype(F32)).astype(BF16)

        return [
            send(ro.at[lax.rem(y + d, NY)], ry.at[d - 1], d, y_peers[d - 1])
            for d in range(1, NY)
        ]

    def forward():
        weights.wait()
        acc[...] = jnp.zeros_like(acc)

        @pl.loop(0, TAPS)
        def _(t):
            start = pl.multiple_of(lax.div(t, 3) * 32, 32)
            acc[...] += dot(bx[0, lax.rem(t, 3), pl.ds(start, 256), :], kv[t])

        out[...] = acc[...].astype(BF16)

    def backward():
        acc[...] = jnp.zeros_like(acc)

        @pl.loop(0, TAPS)
        def _(t):
            start = pl.multiple_of((2 - lax.div(t, 3)) * 32, 32)
            acc[...] += dot_t(gs[2 - lax.rem(t, 3), pl.ds(start, 256), :], kv[t])

        gfeat[...] = acc[...].astype(BF16)

    def y_stage():
        for copy in y_copies:
            copy.wait_recv()

        @pl.loop(0, 36)
        def _(i):
            total = ro[y, i].astype(F32)
            for d in range(NY - 1):
                total += ry[d, i].astype(F32)
            w2[i] = total.astype(BF16)

        return [
            send(w2.at[pl.ds(lax.rem(x + d, NX) * 9, 9)], rx.at[d - 1], 3 + d, x_peers[d - 1])
            for d in range(1, NX)
        ]

    def x_stage():
        for copy in x_copies:
            copy.wait_recv()
        for pair in range(5):
            halves = []
            for t in (2 * pair, 2 * pair + 1):
                if t < TAPS:
                    total = w2[x * 9 + t].astype(F32)
                    for d in range(NX - 1):
                        total += rx[d, t].astype(F32)
                else:
                    total = jnp.zeros((64, LANES), F32)
                halves.append(total)
            turned = jnp.concatenate(halves, axis=0).T.astype(BF16)
            for k in range(NZ):
                wz[k, pair] = turned[k * 16 : (k + 1) * 16, :]
        return [
            send(wz.at[lax.rem(z + d, NZ)], rz.at[d - 1], 6 + d, z_peers[d - 1])
            for d in range(1, NZ)
        ]

    def flip(value, bit):
        return value + bit - 2 * bit * lax.rem(lax.div(value, bit), 2)

    levels = [
        (at(flip(z, 1), x, y, core), lax.rem(z, 2), 0),
        (at(flip(z, 2), x, y, core), lax.rem(lax.div(z, 2), 2), 0),
        (at(flip(z, 4), x, y, core), lax.div(z, 4), 0),
        (core_peer, core, 1),
        (at(z, x, flip(y, 1), core), lax.rem(y, 2), 1),
        (at(z, x, flip(y, 2), core), lax.div(y, 2), 1),
    ]
    for level, (peer, upper, which) in enumerate(levels):
        base = 14 + 10 * level
        slice_copy = send(mo if level == 0 else ma.at[level], mb.at[level], base, peer)
        within = carried_gram(combiner, gram)
        straight = jnp.sum(jnp.where(eye, within, 0.0), axis=0, keepdims=True)
        va[level] = jnp.broadcast_to(straight, (8, RANK))
        da[level] = jnp.where(eye, 0.0, within).astype(BF16)
        gram_copies = [
            send(va.at[level], vb.at[level], base + 1, peer),
            send(da.at[level], db.at[level], base + 2, peer),
        ]
        if level == 0:
            y_copies = core_stage()
            forward()
        if level == 1:
            backward()
        if level == 2:
            x_copies = y_stage()
        if level == 4:
            z_copies = x_stage()
        mix = mixers[which]
        mix = jnp.where(
            upper == 0, mix, jnp.concatenate([mix[:, RANK:], mix[:, :RANK]], axis=1)
        )
        slice_copy.wait_recv()
        shared = 2 * HALF - QUART
        first = dot_t(ma[level, :, :shared], mb[level, :, :shared])
        cross = dot_t(ma[level, :, shared:], mb[level, :, shared:])
        cross = (cross + jnp.where(half == 0, first, 0.0)).astype(BF16)
        po[level] = cross
        cross_copies = [
            send(po.at[level], pr.at[level, k], base + 3 + k, peer)
            for k, peer in enumerate(sum_peers)
        ]
        for copy in gram_copies + cross_copies:
            copy.wait_recv()
        cross = cross.astype(F32)
        for k in range(NX - 1):
            cross += pr[level, k].astype(F32)
        others = pr[level, NX - 1].astype(F32)
        for k in range(NX, len(sum_peers)):
            others += pr[level, k].astype(F32)
        cross += others.T if level == 0 else others
        gm[0:RANK, 0:RANK] = jnp.where(eye, va[level, 0:1], da[level].astype(F32))
        gm[0:RANK, RANK:] = cross
        gm[RANK:, 0:RANK] = cross.T
        gm[RANK:, RANK:] = jnp.where(eye, vb[level, 0:1], db[level].astype(F32))
        gram = gm[...]
        (combiner,) = combiners([gram], mix)
        stacked = jnp.concatenate([ma[level], mb[level]], axis=0)
        ma[level + 1] = dot(combiner, stacked).astype(BF16)

    last = len(levels)
    own_rows = pl.ds(pl.multiple_of(col * 16, 16), 16)
    fr[0] = ma[last, own_rows, :]
    final_copies = [
        send(ma.at[last, own_rows], fr.at[d], 73 + d, x_peers[d - 1]) for d in range(1, NX)
    ]
    for copy in z_copies:
        copy.wait_recv()
    for pair in range(5):
        total = wz[z, pair].astype(F32)
        for d in range(NZ - 1):
            total += rz[d, pair].astype(F32)
        gk[2 * pair] = total[:, :64]
        if 2 * pair + 1 < TAPS:
            gk[2 * pair + 1] = total[:, 64:]
    for copy in final_copies:
        copy.wait_recv()
    k = lax.broadcasted_iota(jnp.int32, (HALF, 144), 0)
    j = lax.broadcasted_iota(jnp.int32, (HALF, 144), 1)
    skip = lax.rem(row, 8) * 144 - half * (QUART - HALF)
    chosen = jnp.where(k == j + skip, 1.0, 0.0).astype(BF16)
    held = fr[lax.rem(x - lax.div(z, 2) + NX, NX)]
    sketch[...] = dot(held, chosen).astype(BF16)
    for copy in started:
        copy.wait_send()


def step_call(feat, grad, kern, proj, mixers):
    vmem = pl.BlockSpec(memory_space=pltpu.VMEM)
    return pl.pallas_call(
        step_kernel,
        in_specs=[pl.BlockSpec(memory_space=pl.ANY)] * 4 + [vmem],
        out_specs=[vmem] * 4,
        out_shape=[
            jax.ShapeDtypeStruct((256, CH), BF16),
            jax.ShapeDtypeStruct((256, CH), BF16),
            jax.ShapeDtypeStruct((TAPS, 16, 64), F32),
            jax.ShapeDtypeStruct((16, 144), BF16),
        ],
        scratch_shapes=[
            pltpu.VMEM((NX, 3, 320, CH), BF16),
            pltpu.VMEM((NX, 2, 16, CH), BF16),
            pltpu.VMEM((NX, RANK, 256), BF16),
            pltpu.VMEM((3, 320, CH), BF16),
            pltpu.VMEM((2, 16, CH), BF16),
            pltpu.VMEM((2, 16, CH), F32),
            pltpu.VMEM((2, 3, 16, CH), BF16),
            pltpu.VMEM((2, 2, 16, CH), F32),
            pltpu.VMEM((3, 320, CH), BF16),
            pltpu.VMEM((CH, 256), BF16),
            pltpu.VMEM((TAPS, CH, CH), BF16),
            pltpu.VMEM((NY, NC, 36, 64, LANES), BF16),
            pltpu.VMEM((256, CH), F32),
            pltpu.VMEM((NY, 36, 64, LANES), BF16),
            pltpu.VMEM((NY, 36, 64, LANES), BF16),
            pltpu.VMEM((NY - 1, 36, 64, LANES), BF16),
            pltpu.VMEM((36, 64, LANES), BF16),
            pltpu.VMEM((NX - 1, 9, 64, LANES), BF16),
            pltpu.VMEM((NZ, 5, 16, LANES), BF16),
            pltpu.VMEM((NZ - 1, 5, 16, LANES), BF16),
            pltpu.VMEM((4, 4, RANK, QUART), BF16),
            pltpu.VMEM((4, 2 * RANK, QUART), BF16),
            pltpu.VMEM((RANK, HALF), BF16),
            pltpu.VMEM((7, RANK, HALF), BF16),
            pltpu.VMEM((6, RANK, HALF), BF16),
            pltpu.VMEM((6, RANK, RANK), BF16),
            pltpu.VMEM((6, RANK, RANK), BF16),
            pltpu.VMEM((6, 8, RANK), F32),
            pltpu.VMEM((6, 8, RANK), F32),
            pltpu.VMEM((6, RANK, RANK), BF16),
            pltpu.VMEM((6, 7, RANK, RANK), BF16),
            pltpu.VMEM((4, 16, HALF), BF16),
            pltpu.VMEM((2 * RANK, 2 * RANK), F32),
            pltpu.SemaphoreType.DMA((4,)),
            pltpu.SemaphoreType.DMA((102,)),
            pltpu.SemaphoreType.DMA((102,)),
        ],
        compiler_params=pltpu.CompilerParams(
            collective_id=0, has_side_effects=True, vmem_limit_bytes=56 << 20
        ),
        name="conv_step",
    )(feat, grad, kern, proj, mixers)


def settle_kernel(*refs):
    sem = refs[-1]
    copies = [
        pltpu.make_async_copy(refs[i], refs[i + 4], sem.at[i]) for i in range(4)
    ]
    for copy in copies:
        copy.start()
    for copy in copies:
        copy.wait()


def settle(results):
    anywhere = [pl.BlockSpec(memory_space=pl.ANY)] * 4
    return pl.pallas_call(
        settle_kernel,
        in_specs=anywhere,
        out_specs=anywhere,
        out_shape=[jax.ShapeDtypeStruct(r.shape, r.dtype) for r in results],
        scratch_shapes=[pltpu.SemaphoreType.DMA((4,))],
        name="results",
    )(*results)


def body(features, kernel, out_grad, projector, mixers):
    shape = features.shape
    channels = shape[2]
    results = step_call(
        features.reshape(-1, channels),
        out_grad.reshape(-1, channels),
        kernel.reshape(TAPS, channels, channels),
        projector,
        mixers,
    )
    output, grad_features, grad_kernel, own_block = settle(results)
    return (output.reshape(shape), grad_features.reshape(shape), grad_kernel, own_block)


def solution(mesh):
    in_specs = (P("rows", "cols", None), P(), P("rows", "cols", None), P("rows", "cols"), P())
    out_specs = (
        P("rows", "cols", None),
        P("rows", "cols", None),
        P(None, "rows", "cols"),
        P("cols", "rows"),
    )
    return jax.shard_map(body, mesh=mesh, in_specs=in_specs, out_specs=out_specs, check_vma=False)
```

```python
import jax
import jax.numpy as jnp
from jax import lax
from jax.experimental import pallas as pl
from jax.experimental.pallas import tpu as pltpu
from jax.sharding import PartitionSpec as P

NS_STEPS = 5
NX, NZ, NY, NC = 4, 8, 4, 2
LANES = 128
CH = 512
RANK = 128
TAPS = 9
QUART = 1152
HALF = 640
MESH = pl.DeviceIdType.MESH
F32 = jnp.float32
BF16 = jnp.bfloat16


def dot(a, b):
    return jnp.dot(a, b, preferred_element_type=F32)


def dot_t(a, b):
    return lax.dot_general(a, b, (((1,), (1,)), ((), ())), preferred_element_type=F32)


def split(v):
    high = v.astype(BF16)
    return high, (v - high.astype(F32)).astype(BF16)


def start_spread(gram):
    size = gram.shape[0]
    i = lax.broadcasted_iota(jnp.int32, (size, size), 0)
    j = lax.broadcasted_iota(jnp.int32, (size, size), 1)
    eye = jnp.where(i == j, 1.0, 0.0)
    trace = jnp.sum(gram * eye, keepdims=True)
    spread = gram / (trace + 1e-06) - eye * (1.0 / size)
    return spread / (jnp.sqrt(jnp.sum(spread * spread, keepdims=True)) + 1e-06)


def combiners(grams, mix):
    spreads = [start_spread(gram) for gram in grams]
    for sweep in range(NS_STEPS - 1):
        rounded = [s.astype(BF16) for s in spreads]
        squares = [dot(r, r).astype(BF16) for r in rounded]
        spreads = [
            1.5 * s - 0.5 * dot(r, q) for s, r, q in zip(spreads, rounded, squares)
        ]
    parts = [split(s) for s in spreads]
    squares = [dot(high, high).astype(BF16) for high, low in parts]
    mixed = [dot(mix, high) + dot(mix, low) for high, low in parts]
    wide = mix.astype(F32)
    return [
        (0.5 * wide + 0.75 * m - 0.25 * dot(m.astype(BF16), q)).astype(BF16)
        for m, q in zip(mixed, squares)
    ]


def carried_gram(combiner, gram):
    high, low = split(gram)
    first = dot(combiner, high) + dot(combiner, low)
    high, low = split(first)
    return dot_t(high, combiner) + dot_t(low, combiner)


def shift_columns(held, edges, slot_at):
    row_in = lax.broadcasted_iota(jnp.int32, (32, CH), 0)
    left, right = edges
    for h in range(10):
        rows = slice(h * 32, h * 32 + 32)
        mid = held[slot_at + (1, rows)].astype(F32)
        before = jnp.where(row_in == 0, left[h : h + 1], pltpu.roll(mid, 1, 0))
        after = jnp.where(row_in == 31, right[h : h + 1], pltpu.roll(mid, 31, 0))
        held[slot_at + (0, rows)] = before.astype(BF16)
        held[slot_at + (2, rows)] = after.astype(BF16)


def step_kernel(
    feat, grad, kern, proj, mixers, out, gfeat, gk, sketch,
    bx, be, pj, gs, strips, cut, edge, line, xsp, ogt, kv, wt, acc,
    ro, rc, ry, w2, rx, wz, rz, m0, m1, mo, ma, mb, da, db, va, vb, po, pr, fr, gm, lsem, ssem, rsem,
):
    row, col = lax.axis_index("rows"), lax.axis_index("cols")
    n_rows, n_cols = NX * NZ, NY * NC
    z, x = lax.div(row, NX), lax.rem(row, NX)
    y, core = lax.div(col, NC), lax.rem(col, NC)

    def at(zz, xx, yy, cc):
        return (zz * NX + xx, yy * NC + cc)

    x_peers = [at(z, lax.rem(x + d, NX), y, core) for d in range(1, NX)]
    y_peers = [at(z, x, lax.rem(y + d, NY), core) for d in range(1, NY)]
    z_peers = [at(lax.rem(z + d, NZ), x, y, core) for d in range(1, NZ)]
    core_peer = at(z, x, y, 1 - core)
    half = lax.rem(z, 2)
    mate = z + 1 - 2 * half
    sum_peers = x_peers + [at(mate, lax.rem(x + d, NX), y, core) for d in range(NX)]
    above, below = lax.rem(row + n_rows - 1, n_rows), lax.rem(row + 1, n_rows)
    before, after = lax.rem(col + n_cols - 1, n_cols), lax.rem(col + 1, n_cols)
    around = [(r, c) for c in (before, after) for r in (above, row, below)]
    around += [(above, col), (below, col)]

    def fetch(src, dst, i):
        copy = pltpu.make_async_copy(src, dst, lsem.at[i])
        copy.start()
        return copy

    own_band = fetch(feat, bx.at[0, 1, 32:288], 0)
    own_grad = fetch(grad, gs.at[1, 32:288], 1)
    own_proj = fetch(proj, pj.at[0], 2)
    weights = fetch(kern, kv, 3)

    barrier = pltpu.get_barrier_semaphore()
    peers = sum_peers + y_peers + z_peers + [core_peer] + around
    for peer in peers:
        pl.semaphore_signal(barrier, inc=1, device_id=peer, device_id_type=MESH)
    own_band.wait()
    own_grad.wait()
    for which, held in enumerate((bx.at[0, 1], gs.at[1])):
        for h in range(8):
            at_row = 8 * which + h
            first = held[32 + h * 32 : 48 + h * 32].astype(F32)
            last = held[48 + h * 32 : 64 + h * 32].astype(F32)
            cut[0, at_row : at_row + 1] = first[0:1]
            cut[1, at_row : at_row + 1] = last[15:16]
    strips[...] = cut[...].astype(BF16)
    pl.semaphore_wait(barrier, len(peers))

    started = []

    def send(src, dst, i, peer):
        copy = pltpu.make_async_remote_copy(
            src_ref=src,
            dst_ref=dst,
            send_sem=ssem.at[i],
            recv_sem=rsem.at[i],
            device_id=peer,
            device_id_type=MESH,
        )
        copy.start()
        started.append(copy)
        return copy

    halo = []
    for k, r in enumerate((below, row, above)):
        halo.append(send(strips.at[0], edge.at[1, k], 77 + k, (r, before)))
        halo.append(send(strips.at[1], edge.at[0, k], 80 + k, (r, after)))
    halo.append(send(feat.at[224:256], bx.at[0, 1, 0:32], 83, (below, col)))
    halo.append(send(feat.at[0:32], bx.at[0, 1, 288:320], 84, (above, col)))
    halo.append(send(grad.at[224:256], gs.at[1, 0:32], 85, (below, col)))
    halo.append(send(grad.at[0:32], gs.at[1, 288:320], 86, (above, col)))
    main = {
        d: (
            send(feat, bx.at[d, 1, 32:288], 86 + d, x_peers[d - 1]),
            send(proj, pj.at[d], 89 + d, x_peers[d - 1]),
        )
        for d in (2, 1, 3)
    }
    own_proj.wait()
    ogt[...] = gs[1, 32:288].astype(F32).T.astype(BF16)
    for copy in halo:
        copy.wait_recv()

    def kept(value, outside):
        return jnp.where(outside, jnp.zeros_like(value), value)

    top, bottom = row == 0, row == n_rows - 1
    for held in (bx.at[0, 1], gs.at[1]):
        held[0:32] = kept(held[0:32], top)
        held[288:320] = kept(held[288:320], bottom)
    line[...] = jnp.zeros_like(line)
    for side, outside in enumerate((col == 0, col == n_cols - 1)):
        up, mid, down = [kept(edge[side, k].astype(F32), outside) for k in range(3)]
        for which in range(2):
            rows = 8 * which
            line[which, side, 0:1] = kept(up[rows + 7 : rows + 8], top)
            line[which, side, 1:9] = mid[rows : rows + 8]
            line[which, side, 9:10] = kept(down[rows : rows + 1], bottom)
    be[0] = line[0].astype(BF16)
    ends = {
        d: (
            send(bx.at[0, 1, 0:32], bx.at[d, 1, 0:32], 92 + d, x_peers[d - 1]),
            send(bx.at[0, 1, 288:320], bx.at[d, 1, 288:320], 95 + d, x_peers[d - 1]),
            send(be.at[0], be.at[d], 98 + d, x_peers[d - 1]),
        )
        for d in (2, 1, 3)
    }
    shift_columns(bx, (line[0, 0], line[0, 1]), (0,))

    ci = lax.broadcasted_iota(jnp.int32, (CH, CH), 0)
    to = lax.broadcasted_iota(jnp.int32, (CH, CH), 1)
    source = lax.rem(lax.div(to, 16), NZ) * 64 + lax.div(to, LANES) * 16 + lax.rem(to, 16)
    perm = jnp.where(ci == source, 1.0, 0.0).astype(BF16)
    for b in range(3):
        xsp[b] = dot(bx[0, b], perm).astype(BF16)

    @pl.loop(0, TAPS)
    def _(t):
        start = pl.multiple_of(lax.div(t, 3) * 32, 32)
        terms = dot(ogt[...], xsp[lax.rem(t, 3), pl.ds(start, 256), :]).astype(BF16)
        for yy in range(NY):
            for cc in range(NC):
                first = (yy * NC + cc) * 64
                for xx in range(NX):
                    wt[yy, cc, xx * TAPS + t] = terms[
                        first : first + 64, xx * LANES : (xx + 1) * LANES
                    ]

    core_copy = send(wt.at[:, 1 - core], rc, 0, core_peer)
    shift_columns(gs, (line[1, 0], line[1, 1]), ())

    def sketch_band(slot):
        j = lax.rem(x - slot + NX, NX)
        p = pj[slot]
        for t in range(TAPS):
            a, b = t // 3, t % 3
            part = dot(p, bx[slot, b, a * 32 : a * 32 + 256, :]).astype(BF16)
            for i in range(4):
                q, lane = (4 * t + i) // 9, (4 * t + i) % 9
                m0[j, q, :, lane * LANES : (lane + 1) * LANES] = part[
                    :, i * LANES : (i + 1) * LANES
                ]

    sketch_band(0)
    for d in (3, 1, 2):
        for copy in main[d] + ends[d]:
            copy.wait_recv()
        edges = be[d].astype(F32)
        shift_columns(bx, (edges[0], edges[1]), (d,))
        sketch_band(d)

    def pair_rows(pair, q):
        return jnp.concatenate([m0[2 * pair, q], m0[2 * pair + 1, q]], axis=0)

    grams = []
    for pair in range(2):
        gram = jnp.zeros((2 * RANK, 2 * RANK), F32)
        for q in range(4):
            stacked = pair_rows(pair, q)
            gram += dot_t(stacked, stacked)
        grams.append(gram)
    for pair, combiner in enumerate(combiners(grams, mixers[0])):
        for q in range(4):
            m1[q, pair * RANK : (pair + 1) * RANK, :] = dot(combiner, pair_rows(pair, q)).astype(
                BF16
            )

    gram = dot_t(m1[0], m1[0])
    for q in range(1, 4):
        gram += dot_t(m1[q], m1[q])
    (combiner,) = combiners([gram], mixers[0])
    merged = dot(combiner, m1[x])
    low, high = merged[:, :HALF], merged[:, QUART - HALF :]
    ma[0] = jnp.where(half == 0, low, high).astype(BF16)
    mo[...] = jnp.where(half == 0, high, low).astype(BF16)
    eye = lax.broadcasted_iota(jnp.int32, (RANK, RANK), 0) == lax.broadcasted_iota(
        jnp.int32, (RANK, RANK), 1
    )

    def core_stage():
        core_copy.wait_recv()

        @pl.loop(0, 36)
        def _(i):
            ro[:, i] = (wt[:, core, i].astype(F32) + rc[:, i].astype(F32)).astype(BF16)

        return [
            send(ro.at[lax.rem(y + d, NY)], ry.at[d - 1], d, y_peers[d - 1])
            for d in range(1, NY)
        ]

    def forward():
        weights.wait()
        acc[...] = jnp.zeros_like(acc)

        @pl.loop(0, TAPS)
        def _(t):
            start = pl.multiple_of(lax.div(t, 3) * 32, 32)
            acc[...] += dot(bx[0, lax.rem(t, 3), pl.ds(start, 256), :], kv[t])

        out[...] = acc[...].astype(BF16)

    def backward():
        acc[...] = jnp.zeros_like(acc)

        @pl.loop(0, TAPS)
        def _(t):
            start = pl.multiple_of((2 - lax.div(t, 3)) * 32, 32)
            acc[...] += dot_t(gs[2 - lax.rem(t, 3), pl.ds(start, 256), :], kv[t])

        gfeat[...] = acc[...].astype(BF16)

    def y_stage():
        for copy in y_copies:
            copy.wait_recv()

        @pl.loop(0, 36)
        def _(i):
            total = ro[y, i].astype(F32)
            for d in range(NY - 1):
                total += ry[d, i].astype(F32)
            w2[i] = total.astype(BF16)

        return [
            send(w2.at[pl.ds(lax.rem(x + d, NX) * 9, 9)], rx.at[d - 1], 3 + d, x_peers[d - 1])
            for d in range(1, NX)
        ]

    def x_stage():
        for copy in x_copies:
            copy.wait_recv()
        for pair in range(5):
            halves = []
            for t in (2 * pair, 2 * pair + 1):
                if t < TAPS:
                    total = w2[x * 9 + t].astype(F32)
                    for d in range(NX - 1):
                        total += rx[d, t].astype(F32)
                else:
                    total = jnp.zeros((64, LANES), F32)
                halves.append(total)
            turned = jnp.concatenate(halves, axis=0).T.astype(BF16)
            for k in range(NZ):
                wz[k, pair] = turned[k * 16 : (k + 1) * 16, :]
        return [
            send(wz.at[lax.rem(z + d, NZ)], rz.at[d - 1], 6 + d, z_peers[d - 1])
            for d in range(1, NZ)
        ]

    def flip(value, bit):
        return value + bit - 2 * bit * lax.rem(lax.div(value, bit), 2)

    levels = [
        (at(flip(z, 1), x, y, core), lax.rem(z, 2), 0),
        (at(flip(z, 2), x, y, core), lax.rem(lax.div(z, 2), 2), 0),
        (at(flip(z, 4), x, y, core), lax.div(z, 4), 0),
        (core_peer, core, 1),
        (at(z, x, flip(y, 1), core), lax.rem(y, 2), 1),
        (at(z, x, flip(y, 2), core), lax.div(y, 2), 1),
    ]
    for level, (peer, upper, which) in enumerate(levels):
        base = 14 + 10 * level
        slice_copy = send(mo if level == 0 else ma.at[level], mb.at[level], base, peer)
        within = carried_gram(combiner, gram)
        straight = jnp.sum(jnp.where(eye, within, 0.0), axis=0, keepdims=True)
        va[level] = jnp.broadcast_to(straight, (8, RANK))
        da[level] = jnp.where(eye, 0.0, within).astype(BF16)
        gram_copies = [
            send(va.at[level], vb.at[level], base + 1, peer),
            send(da.at[level], db.at[level], base + 2, peer),
        ]
        if level == 0:
            y_copies = core_stage()
            forward()
        if level == 1:
            backward()
        if level == 2:
            x_copies = y_stage()
        if level == 4:
            z_copies = x_stage()
        mix = mixers[which]
        mix = jnp.where(
            upper == 0, mix, jnp.concatenate([mix[:, RANK:], mix[:, :RANK]], axis=1)
        )
        slice_copy.wait_recv()
        shared = 2 * HALF - QUART
        first = dot_t(ma[level, :, :shared], mb[level, :, :shared])
        cross = dot_t(ma[level, :, shared:], mb[level, :, shared:])
        cross = (cross + jnp.where(half == 0, first, 0.0)).astype(BF16)
        po[level] = cross
        cross_copies = [
            send(po.at[level], pr.at[level, k], base + 3 + k, peer)
            for k, peer in enumerate(sum_peers)
        ]
        for copy in gram_copies + cross_copies:
            copy.wait_recv()
        cross = cross.astype(F32)
        for k in range(NX - 1):
            cross += pr[level, k].astype(F32)
        others = pr[level, NX - 1].astype(F32)
        for k in range(NX, len(sum_peers)):
            others += pr[level, k].astype(F32)
        cross += others.T if level == 0 else others
        gm[0:RANK, 0:RANK] = jnp.where(eye, va[level, 0:1], da[level].astype(F32))
        gm[0:RANK, RANK:] = cross
        gm[RANK:, 0:RANK] = cross.T
        gm[RANK:, RANK:] = jnp.where(eye, vb[level, 0:1], db[level].astype(F32))
        gram = gm[...]
        (combiner,) = combiners([gram], mix)
        stacked = jnp.concatenate([ma[level], mb[level]], axis=0)
        ma[level + 1] = dot(combiner, stacked).astype(BF16)

    last = len(levels)
    own_rows = pl.ds(pl.multiple_of(col * 16, 16), 16)
    fr[0] = ma[last, own_rows, :]
    final_copies = [
        send(ma.at[last, own_rows], fr.at[d], 73 + d, x_peers[d - 1]) for d in range(1, NX)
    ]
    for copy in z_copies:
        copy.wait_recv()
    for pair in range(5):
        total = wz[z, pair].astype(F32)
        for d in range(NZ - 1):
            total += rz[d, pair].astype(F32)
        gk[2 * pair] = total[:, :64]
        if 2 * pair + 1 < TAPS:
            gk[2 * pair + 1] = total[:, 64:]
    for copy in final_copies:
        copy.wait_recv()
    k = lax.broadcasted_iota(jnp.int32, (HALF, 144), 0)
    j = lax.broadcasted_iota(jnp.int32, (HALF, 144), 1)
    skip = lax.rem(row, 8) * 144 - half * (QUART - HALF)
    chosen = jnp.where(k == j + skip, 1.0, 0.0).astype(BF16)
    held = fr[lax.rem(x - lax.div(z, 2) + NX, NX)]
    sketch[...] = dot(held, chosen).astype(BF16)
    for copy in started:
        copy.wait_send()


def step_call(feat, grad, kern, proj, mixers):
    vmem = pl.BlockSpec(memory_space=pltpu.VMEM)
    return pl.pallas_call(
        step_kernel,
        in_specs=[pl.BlockSpec(memory_space=pl.ANY)] * 4 + [vmem],
        out_specs=[vmem] * 4,
        out_shape=[
            jax.ShapeDtypeStruct((256, CH), BF16),
            jax.ShapeDtypeStruct((256, CH), BF16),
            jax.ShapeDtypeStruct((TAPS, 16, 64), F32),
            jax.ShapeDtypeStruct((16, 144), BF16),
        ],
        scratch_shapes=[
            pltpu.VMEM((NX, 3, 320, CH), BF16),
            pltpu.VMEM((NX, 2, 16, CH), BF16),
            pltpu.VMEM((NX, RANK, 256), BF16),
            pltpu.VMEM((3, 320, CH), BF16),
            pltpu.VMEM((2, 16, CH), BF16),
            pltpu.VMEM((2, 16, CH), F32),
            pltpu.VMEM((2, 3, 16, CH), BF16),
            pltpu.VMEM((2, 2, 16, CH), F32),
            pltpu.VMEM((3, 320, CH), BF16),
            pltpu.VMEM((CH, 256), BF16),
            pltpu.VMEM((TAPS, CH, CH), BF16),
            pltpu.VMEM((NY, NC, 36, 64, LANES), BF16),
            pltpu.VMEM((256, CH), F32),
            pltpu.VMEM((NY, 36, 64, LANES), BF16),
            pltpu.VMEM((NY, 36, 64, LANES), BF16),
            pltpu.VMEM((NY - 1, 36, 64, LANES), BF16),
            pltpu.VMEM((36, 64, LANES), BF16),
            pltpu.VMEM((NX - 1, 9, 64, LANES), BF16),
            pltpu.VMEM((NZ, 5, 16, LANES), BF16),
            pltpu.VMEM((NZ - 1, 5, 16, LANES), BF16),
            pltpu.VMEM((4, 4, RANK, QUART), BF16),
            pltpu.VMEM((4, 2 * RANK, QUART), BF16),
            pltpu.VMEM((RANK, HALF), BF16),
            pltpu.VMEM((7, RANK, HALF), BF16),
            pltpu.VMEM((6, RANK, HALF), BF16),
            pltpu.VMEM((6, RANK, RANK), BF16),
            pltpu.VMEM((6, RANK, RANK), BF16),
            pltpu.VMEM((6, 8, RANK), F32),
            pltpu.VMEM((6, 8, RANK), F32),
            pltpu.VMEM((6, RANK, RANK), BF16),
            pltpu.VMEM((6, 7, RANK, RANK), BF16),
            pltpu.VMEM((4, 16, HALF), BF16),
            pltpu.VMEM((2 * RANK, 2 * RANK), F32),
            pltpu.SemaphoreType.DMA((4,)),
            pltpu.SemaphoreType.DMA((102,)),
            pltpu.SemaphoreType.DMA((102,)),
        ],
        compiler_params=pltpu.CompilerParams(
            collective_id=0, has_side_effects=True, vmem_limit_bytes=56 << 20
        ),
        name="conv_step",
    )(feat, grad, kern, proj, mixers)


def settle_kernel(*refs):
    for held, result in zip(refs[:4], refs[4:]):
        result[...] = held[...]


def settle(results):
    vmem = [pl.BlockSpec(memory_space=pltpu.VMEM)] * 4
    return pl.pallas_call(
        settle_kernel,
        in_specs=vmem,
        out_specs=vmem,
        out_shape=[jax.ShapeDtypeStruct(r.shape, r.dtype) for r in results],
        name="results",
    )(*results)


def body(features, kernel, out_grad, projector, mixers):
    shape = features.shape
    channels = shape[2]
    results = step_call(
        features.reshape(-1, channels),
        out_grad.reshape(-1, channels),
        kernel.reshape(TAPS, channels, channels),
        projector,
        mixers,
    )
    output, grad_features, grad_kernel, own_block = settle(results)
    return (output.reshape(shape), grad_features.reshape(shape), grad_kernel, own_block)


def solution(mesh):
    in_specs = (P("rows", "cols", None), P(), P("rows", "cols", None), P("rows", "cols"), P())
    out_specs = (
        P("rows", "cols", None),
        P("rows", "cols", None),
        P(None, "rows", "cols"),
        P("cols", "rows"),
    )
    return jax.shard_map(body, mesh=mesh, in_specs=in_specs, out_specs=out_specs, check_vma=False)
```

```python
import jax
import jax.numpy as jnp
from jax import lax
from jax.experimental import pallas as pl
from jax.experimental.pallas import tpu as pltpu
from jax.sharding import PartitionSpec as P

NS_STEPS = 5
NX, NZ, NY, NC = 4, 8, 4, 2
LANES = 128
CH = 512
RANK = 128
TAPS = 9
QUART = 1152
HALF = 640
FAR_FIRST = (4, 3, 5, 6, 1, 0, 2)
MESH = pl.DeviceIdType.MESH
F32 = jnp.float32
BF16 = jnp.bfloat16


def dot(a, b):
    return jnp.dot(a, b, preferred_element_type=F32)


def dot_t(a, b):
    return lax.dot_general(a, b, (((1,), (1,)), ((), ())), preferred_element_type=F32)


def split(v):
    high = v.astype(BF16)
    return high, (v - high.astype(F32)).astype(BF16)


def start_spread(gram):
    size = gram.shape[0]
    i = lax.broadcasted_iota(jnp.int32, (size, size), 0)
    j = lax.broadcasted_iota(jnp.int32, (size, size), 1)
    eye = jnp.where(i == j, 1.0, 0.0)
    trace = jnp.sum(gram * eye, keepdims=True)
    spread = gram / (trace + 1e-06) - eye * (1.0 / size)
    return spread, jnp.sum(spread * spread, keepdims=True)


def combined(spread, squared_norm, mix):
    scale = 1.0 / (jnp.sqrt(squared_norm) + 1e-06)
    rounded = spread.astype(BF16)
    cubed = dot(rounded, dot(rounded, rounded).astype(BF16))
    spread = (1.5 * scale) * spread - (0.5 * scale * scale * scale) * cubed
    for sweep in range(NS_STEPS - 2):
        rounded = spread.astype(BF16)
        square = dot(rounded, rounded).astype(BF16)
        spread = 1.5 * spread - 0.5 * dot(rounded, square)
    high, low = split(spread)
    square = dot(high, high).astype(BF16)
    mixed = dot(mix, high) + dot(mix, low)
    wide = 0.5 * mix.astype(F32) + 0.75 * mixed
    return (wide - 0.25 * dot(mixed.astype(BF16), square)).astype(BF16)


def carried_gram(combiner, gram):
    high, low = split(gram)
    first = dot(combiner, high) + dot(combiner, low)
    high, low = split(first)
    return dot_t(high, combiner) + dot_t(low, combiner)


def shift_columns(held, edges, slot_at):
    row_in = lax.broadcasted_iota(jnp.int32, (32, CH), 0)
    left, right = edges
    for h in range(10):
        rows = slice(h * 32, h * 32 + 32)
        mid = held[slot_at + (1, rows)].astype(F32)
        before = jnp.where(row_in == 0, left[h : h + 1], pltpu.roll(mid, 1, 0))
        after = jnp.where(row_in == 31, right[h : h + 1], pltpu.roll(mid, 31, 0))
        held[slot_at + (0, rows)] = before.astype(BF16)
        held[slot_at + (2, rows)] = after.astype(BF16)


def step_kernel(
    feat, grad, kern, proj, mixers, out, gfeat, gk, sketch,
    bx, be, pj, gs, strips, cut, edge, line, xsp, ogt, kv, wt, acc,
    ro, rc, ry, w2, rx, wz, rz, m0, m1, mo, ma, mb, da, db, va, vb, po, pr, fr, gm, ym, lsem, ssem, rsem,
):
    row, col = lax.axis_index("rows"), lax.axis_index("cols")
    n_rows, n_cols = NX * NZ, NY * NC
    z, x = lax.div(row, NX), lax.rem(row, NX)
    y, core = lax.div(col, NC), lax.rem(col, NC)

    def at(zz, xx, yy, cc):
        return (zz * NX + xx, yy * NC + cc)

    x_peers = [at(z, lax.rem(x + d, NX), y, core) for d in range(1, NX)]
    y_peers = [at(z, x, lax.rem(y + d, NY), core) for d in range(1, NY)]
    z_peers = [at(lax.rem(z + d, NZ), x, y, core) for d in range(1, NZ)]
    core_peer = at(z, x, y, 1 - core)
    half = lax.rem(z, 2)
    mate = z + 1 - 2 * half
    sum_peers = x_peers + [at(mate, lax.rem(x + d, NX), y, core) for d in range(NX)]
    above, below = lax.rem(row + n_rows - 1, n_rows), lax.rem(row + 1, n_rows)
    before, after = lax.rem(col + n_cols - 1, n_cols), lax.rem(col + 1, n_cols)
    around = [(r, c) for c in (before, after) for r in (above, row, below)]
    around += [(above, col), (below, col)]

    def fetch(src, dst, i):
        copy = pltpu.make_async_copy(src, dst, lsem.at[i])
        copy.start()
        return copy

    own_band = fetch(feat, bx.at[0, 1, 32:288], 0)
    own_grad = fetch(grad, gs.at[1, 32:288], 1)
    own_proj = fetch(proj, pj.at[0], 2)
    weights = fetch(kern, kv, 3)

    barrier = pltpu.get_barrier_semaphore()
    peers = sum_peers + y_peers + z_peers + [core_peer] + around
    for peer in peers:
        pl.semaphore_signal(barrier, inc=1, device_id=peer, device_id_type=MESH)
    own_band.wait()
    own_grad.wait()
    for which, held in enumerate((bx.at[0, 1], gs.at[1])):
        for h in range(8):
            at_row = 8 * which + h
            first = held[32 + h * 32 : 48 + h * 32].astype(F32)
            last = held[48 + h * 32 : 64 + h * 32].astype(F32)
            cut[0, at_row : at_row + 1] = first[0:1]
            cut[1, at_row : at_row + 1] = last[15:16]
    strips[...] = cut[...].astype(BF16)
    pl.semaphore_wait(barrier, len(peers))

    started = []

    def send(src, dst, i, peer):
        copy = pltpu.make_async_remote_copy(
            src_ref=src,
            dst_ref=dst,
            send_sem=ssem.at[i],
            recv_sem=rsem.at[i],
            device_id=peer,
            device_id_type=MESH,
        )
        copy.start()
        started.append(copy)
        return copy

    halo = []
    for k, r in enumerate((below, row, above)):
        halo.append(send(strips.at[0], edge.at[1, k], 77 + k, (r, before)))
        halo.append(send(strips.at[1], edge.at[0, k], 80 + k, (r, after)))
    halo.append(send(feat.at[224:256], bx.at[0, 1, 0:32], 83, (below, col)))
    halo.append(send(feat.at[0:32], bx.at[0, 1, 288:320], 84, (above, col)))
    halo.append(send(grad.at[224:256], gs.at[1, 0:32], 85, (below, col)))
    halo.append(send(grad.at[0:32], gs.at[1, 288:320], 86, (above, col)))
    main = {
        d: (
            send(feat, bx.at[d, 1, 32:288], 86 + d, x_peers[d - 1]),
            send(proj, pj.at[d], 89 + d, x_peers[d - 1]),
        )
        for d in (2, 1, 3)
    }
    own_proj.wait()
    ogt[...] = gs[1, 32:288].astype(F32).T.astype(BF16)
    for copy in halo:
        copy.wait_recv()

    def kept(value, outside):
        return jnp.where(outside, jnp.zeros_like(value), value)

    top, bottom = row == 0, row == n_rows - 1
    for held in (bx.at[0, 1], gs.at[1]):
        held[0:32] = kept(held[0:32], top)
        held[288:320] = kept(held[288:320], bottom)
    line[...] = jnp.zeros_like(line)
    for side, outside in enumerate((col == 0, col == n_cols - 1)):
        up, mid, down = [kept(edge[side, k].astype(F32), outside) for k in range(3)]
        for which in range(2):
            rows = 8 * which
            line[which, side, 0:1] = kept(up[rows + 7 : rows + 8], top)
            line[which, side, 1:9] = mid[rows : rows + 8]
            line[which, side, 9:10] = kept(down[rows : rows + 1], bottom)
    be[0] = line[0].astype(BF16)
    ends = {
        d: (
            send(bx.at[0, 1, 0:32], bx.at[d, 1, 0:32], 92 + d, x_peers[d - 1]),
            send(bx.at[0, 1, 288:320], bx.at[d, 1, 288:320], 95 + d, x_peers[d - 1]),
            send(be.at[0], be.at[d], 98 + d, x_peers[d - 1]),
        )
        for d in (2, 1, 3)
    }
    shift_columns(bx, (line[0, 0], line[0, 1]), (0,))

    ci = lax.broadcasted_iota(jnp.int32, (CH, CH), 0)
    to = lax.broadcasted_iota(jnp.int32, (CH, CH), 1)
    source = lax.rem(lax.div(to, 16), NZ) * 64 + lax.div(to, LANES) * 16 + lax.rem(to, 16)
    perm = jnp.where(ci == source, 1.0, 0.0).astype(BF16)
    for b in range(3):
        xsp[b] = dot(bx[0, b], perm).astype(BF16)

    @pl.loop(0, TAPS)
    def _(t):
        start = pl.multiple_of(lax.div(t, 3) * 32, 32)
        terms = dot(ogt[...], xsp[lax.rem(t, 3), pl.ds(start, 256), :]).astype(BF16)
        for yy in range(NY):
            for cc in range(NC):
                first = (yy * NC + cc) * 64
                for xx in range(NX):
                    wt[yy, cc, xx * TAPS + t] = terms[
                        first : first + 64, xx * LANES : (xx + 1) * LANES
                    ]

    core_copy = send(wt.at[:, 1 - core], rc, 0, core_peer)
    shift_columns(gs, (line[1, 0], line[1, 1]), ())

    def sketch_band(slot):
        j = lax.rem(x - slot + NX, NX)
        p = pj[slot]
        for t in range(TAPS):
            a, b = t // 3, t % 3
            part = dot(p, bx[slot, b, a * 32 : a * 32 + 256, :]).astype(BF16)
            for i in range(4):
                q, lane = (4 * t + i) // 9, (4 * t + i) % 9
                m0[j, q, :, lane * LANES : (lane + 1) * LANES] = part[
                    :, i * LANES : (i + 1) * LANES
                ]

    def receive_band(d):
        for copy in main[d] + ends[d]:
            copy.wait_recv()
        edges = be[d].astype(F32)
        shift_columns(bx, (edges[0], edges[1]), (d,))
        sketch_band(d)

    def merge_pair(pair):
        gram = jnp.zeros((2 * RANK, 2 * RANK), F32)
        for q in range(4):
            stacked = jnp.concatenate([m0[2 * pair, q], m0[2 * pair + 1, q]], axis=0)
            gram += dot_t(stacked, stacked)
        combiner = combined(*start_spread(gram), mixers[0])
        for q in range(4):
            stacked = jnp.concatenate([m0[2 * pair, q], m0[2 * pair + 1, q]], axis=0)
            m1[pair, q] = dot(combiner, stacked).astype(BF16)

    sketch_band(0)
    receive_band(3)
    receive_band(1)
    merge_pair(lax.div(x, 2))
    receive_band(2)
    merge_pair(1 - lax.div(x, 2))

    def quarter(q):
        return jnp.concatenate([m1[0, q], m1[1, q]], axis=0)

    gram = jnp.zeros((2 * RANK, 2 * RANK), F32)
    for q in range(4):
        stacked = quarter(q)
        gram += dot_t(stacked, stacked)
    combiner = combined(*start_spread(gram), mixers[0])
    merged = dot(combiner, quarter(x))
    low, high = merged[:, :HALF], merged[:, QUART - HALF :]
    ma[0] = jnp.where(half == 0, low, high).astype(BF16)
    mo[...] = jnp.where(half == 0, high, low).astype(BF16)
    eye = lax.broadcasted_iota(jnp.int32, (RANK, RANK), 0) == lax.broadcasted_iota(
        jnp.int32, (RANK, RANK), 1
    )

    def core_stage():
        core_copy.wait_recv()

        @pl.loop(0, 36)
        def _(i):
            ro[:, i] = (wt[:, core, i].astype(F32) + rc[:, i].astype(F32)).astype(BF16)

        return [
            send(ro.at[lax.rem(y + d, NY)], ry.at[d - 1], d, y_peers[d - 1])
            for d in range(1, NY)
        ]

    def forward():
        weights.wait()
        acc[...] = jnp.zeros_like(acc)

        @pl.loop(0, TAPS)
        def _(t):
            start = pl.multiple_of(lax.div(t, 3) * 32, 32)
            acc[...] += dot(bx[0, lax.rem(t, 3), pl.ds(start, 256), :], kv[t])

        out[...] = acc[...].astype(BF16)

    def backward():
        acc[...] = jnp.zeros_like(acc)

        @pl.loop(0, TAPS)
        def _(t):
            start = pl.multiple_of((2 - lax.div(t, 3)) * 32, 32)
            acc[...] += dot_t(gs[2 - lax.rem(t, 3), pl.ds(start, 256), :], kv[t])

        gfeat[...] = acc[...].astype(BF16)

    def y_stage():
        for copy in y_copies:
            copy.wait_recv()

        @pl.loop(0, 36)
        def _(i):
            total = ro[y, i].astype(F32)
            for d in range(NY - 1):
                total += ry[d, i].astype(F32)
            w2[i] = total.astype(BF16)

        return [
            send(w2.at[pl.ds(lax.rem(x + d, NX) * 9, 9)], rx.at[d - 1], 3 + d, x_peers[d - 1])
            for d in range(1, NX)
        ]

    def x_stage():
        for copy in x_copies:
            copy.wait_recv()
        for pair in range(5):
            halves = []
            for t in (2 * pair, 2 * pair + 1):
                if t < TAPS:
                    total = w2[x * 9 + t].astype(F32)
                    for d in range(NX - 1):
                        total += rx[d, t].astype(F32)
                else:
                    total = jnp.zeros((64, LANES), F32)
                halves.append(total)
            turned = jnp.concatenate(halves, axis=0).T.astype(BF16)
            for k in range(NZ):
                wz[k, pair] = turned[k * 16 : (k + 1) * 16, :]
        return [
            send(wz.at[lax.rem(z + d, NZ)], rz.at[d - 1], 6 + d, z_peers[d - 1])
            for d in range(1, NZ)
        ]

    def flip(value, bit):
        return value + bit - 2 * bit * lax.rem(lax.div(value, bit), 2)

    levels = [
        (at(flip(z, 1), x, y, core), lax.rem(z, 2), 0),
        (at(flip(z, 2), x, y, core), lax.rem(lax.div(z, 2), 2), 0),
        (at(flip(z, 4), x, y, core), lax.div(z, 4), 0),
        (core_peer, core, 1),
        (at(z, x, flip(y, 1), core), lax.rem(y, 2), 1),
        (at(z, x, flip(y, 2), core), lax.div(y, 2), 1),
    ]
    for level, (peer, upper, which) in enumerate(levels):
        base = 14 + 10 * level
        slice_copy = send(mo if level == 0 else ma.at[level], mb.at[level], base, peer)
        within = carried_gram(combiner, gram if level == 0 else gm[...])
        straight = jnp.sum(jnp.where(eye, within, 0.0), axis=0, keepdims=True)
        va[level] = jnp.broadcast_to(straight, (8, RANK))
        da[level] = jnp.where(eye, 0.0, within).astype(BF16)
        gram_copies = [
            send(va.at[level], vb.at[level], base + 1, peer),
            send(da.at[level], db.at[level], base + 2, peer),
        ]
        if level == 0:
            y_copies = core_stage()
        if level == 1:
            forward()
        if level == 2:
            backward()
            x_copies = y_stage()
        if level == 4:
            z_copies = x_stage()
        mix = mixers[which]
        mix = jnp.where(
            upper == 0, mix, jnp.concatenate([mix[:, RANK:], mix[:, :RANK]], axis=1)
        )
        slice_copy.wait_recv()
        shared = 2 * HALF - QUART
        first = dot_t(ma[level, :, :shared], mb[level, :, :shared])
        cross = dot_t(ma[level, :, shared:], mb[level, :, shared:])
        cross = (cross + jnp.where(half == 0, first, 0.0)).astype(BF16)
        po[level] = cross
        cross_copies = [
            send(po.at[level], pr.at[level, k], base + 3 + k, peer)
            for k, peer in sorted(enumerate(sum_peers), key=lambda item: FAR_FIRST[item[0]])
        ]
        for copy in gram_copies:
            copy.wait_recv()
        trace = jnp.sum(va[level, 0:1] + vb[level, 0:1], keepdims=True) + 1e-06
        squared_norm = jnp.zeros((1, 1), F32)
        for k, (straight, rest) in enumerate(((va, da), (vb, db))):
            part = slice(k * RANK, (k + 1) * RANK)
            within = jnp.where(eye, straight[level, 0:1], rest[level].astype(F32))
            gm[part, part] = within
            within = within / trace - jnp.where(eye, 0.5 / RANK, 0.0)
            ym[part, part] = within
            squared_norm += jnp.sum(within * within, keepdims=True)
        for copy in cross_copies:
            copy.wait_recv()
        cross = cross.astype(F32)
        for k in range(NX - 1):
            cross += pr[level, k].astype(F32)
        others = pr[level, NX - 1].astype(F32)
        for k in range(NX, len(sum_peers)):
            others += pr[level, k].astype(F32)
        cross += others.T if level == 0 else others
        scaled = cross / trace
        ym[0:RANK, RANK:] = scaled
        ym[RANK:, 0:RANK] = scaled.T
        squared_norm += 2.0 * jnp.sum(scaled * scaled, keepdims=True)
        combiner = combined(ym[...], squared_norm, mix)
        stacked = jnp.concatenate([ma[level], mb[level]], axis=0)
        ma[level + 1] = dot(combiner, stacked).astype(BF16)
        gm[0:RANK, RANK:] = cross
        gm[RANK:, 0:RANK] = cross.T

    last = len(levels)
    own_rows = pl.ds(pl.multiple_of(col * 16, 16), 16)
    fr[0] = ma[last, own_rows, :]
    final_copies = [
        send(ma.at[last, own_rows], fr.at[d], 73 + d, x_peers[d - 1]) for d in range(1, NX)
    ]
    for copy in z_copies:
        copy.wait_recv()
    for pair in range(5):
        total = wz[z, pair].astype(F32)
        for d in range(NZ - 1):
            total += rz[d, pair].astype(F32)
        gk[2 * pair] = total[:, :64]
        if 2 * pair + 1 < TAPS:
            gk[2 * pair + 1] = total[:, 64:]
    for copy in final_copies:
        copy.wait_recv()
    k = lax.broadcasted_iota(jnp.int32, (HALF, 144), 0)
    j = lax.broadcasted_iota(jnp.int32, (HALF, 144), 1)
    skip = lax.rem(row, 8) * 144 - half * (QUART - HALF)
    chosen = jnp.where(k == j + skip, 1.0, 0.0).astype(BF16)
    held = fr[lax.rem(x - lax.div(z, 2) + NX, NX)]
    sketch[...] = dot(held, chosen).astype(BF16)
    for copy in started:
        copy.wait_send()


def step_call(feat, grad, kern, proj, mixers):
    vmem = pl.BlockSpec(memory_space=pltpu.VMEM)
    return pl.pallas_call(
        step_kernel,
        in_specs=[pl.BlockSpec(memory_space=pl.ANY)] * 4 + [vmem],
        out_specs=[vmem] * 4,
        out_shape=[
            pltpu.VMEM((256, CH), BF16),
            pltpu.VMEM((256, CH), BF16),
            pltpu.VMEM((TAPS, 16, 64), F32),
            pltpu.VMEM((16, 144), BF16),
        ],
        scratch_shapes=[
            pltpu.VMEM((NX, 3, 320, CH), BF16),
            pltpu.VMEM((NX, 2, 16, CH), BF16),
            pltpu.VMEM((NX, RANK, 256), BF16),
            pltpu.VMEM((3, 320, CH), BF16),
            pltpu.VMEM((2, 16, CH), BF16),
            pltpu.VMEM((2, 16, CH), F32),
            pltpu.VMEM((2, 3, 16, CH), BF16),
            pltpu.VMEM((2, 2, 16, CH), F32),
            pltpu.VMEM((3, 320, CH), BF16),
            pltpu.VMEM((CH, 256), BF16),
            pltpu.VMEM((TAPS, CH, CH), BF16),
            pltpu.VMEM((NY, NC, 36, 64, LANES), BF16),
            pltpu.VMEM((256, CH), F32),
            pltpu.VMEM((NY, 36, 64, LANES), BF16),
            pltpu.VMEM((NY, 36, 64, LANES), BF16),
            pltpu.VMEM((NY - 1, 36, 64, LANES), BF16),
            pltpu.VMEM((36, 64, LANES), BF16),
            pltpu.VMEM((NX - 1, 9, 64, LANES), BF16),
            pltpu.VMEM((NZ, 5, 16, LANES), BF16),
            pltpu.VMEM((NZ - 1, 5, 16, LANES), BF16),
            pltpu.VMEM((4, 4, RANK, QUART), BF16),
            pltpu.VMEM((2, 4, RANK, QUART), BF16),
            pltpu.VMEM((RANK, HALF), BF16),
            pltpu.VMEM((7, RANK, HALF), BF16),
            pltpu.VMEM((6, RANK, HALF), BF16),
            pltpu.VMEM((6, RANK, RANK), BF16),
            pltpu.VMEM((6, RANK, RANK), BF16),
            pltpu.VMEM((6, 8, RANK), F32),
            pltpu.VMEM((6, 8, RANK), F32),
            pltpu.VMEM((6, RANK, RANK), BF16),
            pltpu.VMEM((6, 7, RANK, RANK), BF16),
            pltpu.VMEM((4, 16, HALF), BF16),
            pltpu.VMEM((2 * RANK, 2 * RANK), F32),
            pltpu.VMEM((2 * RANK, 2 * RANK), F32),
            pltpu.SemaphoreType.DMA((4,)),
            pltpu.SemaphoreType.DMA((102,)),
            pltpu.SemaphoreType.DMA((102,)),
        ],
        compiler_params=pltpu.CompilerParams(
            collective_id=0, has_side_effects=True, vmem_limit_bytes=56 << 20
        ),
        name="conv_step",
    )(feat, grad, kern, proj, mixers)


def settle_kernel(*refs):
    for held, result in zip(refs[:4], refs[4:]):
        result[...] = held[...]


def settle(results):
    vmem = [pl.BlockSpec(memory_space=pltpu.VMEM)] * 4
    return pl.pallas_call(
        settle_kernel,
        in_specs=vmem,
        out_specs=vmem,
        out_shape=[jax.ShapeDtypeStruct(r.shape, r.dtype) for r in results],
        name="results",
    )(*[pltpu.with_memory_space_constraint(r, pltpu.VMEM) for r in results])


def body(features, kernel, out_grad, projector, mixers):
    shape = features.shape
    channels = shape[2]
    results = step_call(
        features.reshape(-1, channels),
        out_grad.reshape(-1, channels),
        kernel.reshape(TAPS, channels, channels),
        projector,
        mixers,
    )
    output, grad_features, grad_kernel, own_block = settle(results)
    return (output.reshape(shape), grad_features.reshape(shape), grad_kernel, own_block)


def solution(mesh):
    in_specs = (P("rows", "cols", None), P(), P("rows", "cols", None), P("rows", "cols"), P())
    out_specs = (
        P("rows", "cols", None),
        P("rows", "cols", None),
        P(None, "rows", "cols"),
        P("cols", "rows"),
    )
    return jax.shard_map(body, mesh=mesh, in_specs=in_specs, out_specs=out_specs, check_vma=False)
```

```python
import jax
import jax.numpy as jnp
from jax import lax
from jax.experimental import pallas as pl
from jax.experimental.pallas import tpu as pltpu
from jax.sharding import PartitionSpec as P

NS_STEPS = 5
NX, NZ, NY, NC = 4, 8, 4, 2
LANES = 128
CH = 512
RANK = 128
TAPS = 9
QUART = 1152
HALF = 640
FAR_FIRST = (4, 3, 5, 6, 1, 0, 2)
MESH = pl.DeviceIdType.MESH
F32 = jnp.float32
BF16 = jnp.bfloat16


def dot(a, b):
    return jnp.dot(a, b, preferred_element_type=F32)


def dot_t(a, b):
    return lax.dot_general(a, b, (((1,), (1,)), ((), ())), preferred_element_type=F32)


def split(v):
    high = v.astype(BF16)
    return high, (v - high.astype(F32)).astype(BF16)


def start_spread(gram):
    size = gram.shape[0]
    i = lax.broadcasted_iota(jnp.int32, (size, size), 0)
    j = lax.broadcasted_iota(jnp.int32, (size, size), 1)
    eye = jnp.where(i == j, 1.0, 0.0)
    trace = jnp.sum(gram * eye, keepdims=True)
    spread = gram / (trace + 1e-06) - eye * (1.0 / size)
    return spread, jnp.sum(spread * spread, keepdims=True)


def combined(starts, mix):
    spreads = []
    for spread, squared_norm in starts:
        scale = 1.0 / (jnp.sqrt(squared_norm) + 1e-06)
        rounded = spread.astype(BF16)
        cubed = dot(rounded, dot(rounded, rounded).astype(BF16))
        spreads.append(
            (1.5 * scale) * spread - (0.5 * scale * scale * scale) * cubed
        )
    for sweep in range(NS_STEPS - 2):
        rounded = [s.astype(BF16) for s in spreads]
        squares = [dot(r, r).astype(BF16) for r in rounded]
        spreads = [1.5 * s - 0.5 * dot(r, q) for s, r, q in zip(spreads, rounded, squares)]
    parts = [split(s) for s in spreads]
    squares = [dot(high, high).astype(BF16) for high, low in parts]
    mixed = [dot(mix, high) + dot(mix, low) for high, low in parts]
    wide = 0.5 * mix.astype(F32)
    return [
        (wide + 0.75 * m - 0.25 * dot(m.astype(BF16), q)).astype(BF16)
        for m, q in zip(mixed, squares)
    ]


def carried_gram(combiner, gram):
    high, low = split(gram)
    first = dot(combiner, high) + dot(combiner, low)
    high, low = split(first)
    return dot_t(high, combiner) + dot_t(low, combiner)


def shift_columns(held, edges, slot_at):
    row_in = lax.broadcasted_iota(jnp.int32, (32, CH), 0)
    left, right = edges
    for h in range(10):
        rows = slice(h * 32, h * 32 + 32)
        mid = held[slot_at + (1, rows)].astype(F32)
        before = jnp.where(row_in == 0, left[h : h + 1], pltpu.roll(mid, 1, 0))
        after = jnp.where(row_in == 31, right[h : h + 1], pltpu.roll(mid, 31, 0))
        held[slot_at + (0, rows)] = before.astype(BF16)
        held[slot_at + (2, rows)] = after.astype(BF16)


def step_kernel(
    feat, grad, kern, proj, mixers, out, gfeat, gk, sketch,
    bx, be, pj, gs, strips, cut, edge, line, xsp, ogt, kv, wt, acc,
    ro, rc, ry, w2, rx, wz, rz, m0, m1, mo, ma, mb, da, db, va, vb, po, pr, fr, gm, ym, lsem, ssem, rsem,
):
    row, col = lax.axis_index("rows"), lax.axis_index("cols")
    n_rows, n_cols = NX * NZ, NY * NC
    z, x = lax.div(row, NX), lax.rem(row, NX)
    y, core = lax.div(col, NC), lax.rem(col, NC)

    def at(zz, xx, yy, cc):
        return (zz * NX + xx, yy * NC + cc)

    x_peers = [at(z, lax.rem(x + d, NX), y, core) for d in range(1, NX)]
    y_peers = [at(z, x, lax.rem(y + d, NY), core) for d in range(1, NY)]
    z_peers = [at(lax.rem(z + d, NZ), x, y, core) for d in range(1, NZ)]
    core_peer = at(z, x, y, 1 - core)
    half = lax.rem(z, 2)
    mate = z + 1 - 2 * half
    sum_peers = x_peers + [at(mate, lax.rem(x + d, NX), y, core) for d in range(NX)]
    above, below = lax.rem(row + n_rows - 1, n_rows), lax.rem(row + 1, n_rows)
    before, after = lax.rem(col + n_cols - 1, n_cols), lax.rem(col + 1, n_cols)
    around = [(r, c) for c in (before, after) for r in (above, row, below)]
    around += [(above, col), (below, col)]

    def fetch(src, dst, i):
        copy = pltpu.make_async_copy(src, dst, lsem.at[i])
        copy.start()
        return copy

    own_band = fetch(feat, bx.at[0, 1, 32:288], 0)
    own_grad = fetch(grad, gs.at[1, 32:288], 1)
    own_proj = fetch(proj, pj.at[0], 2)
    weights = fetch(kern, kv, 3)

    barrier = pltpu.get_barrier_semaphore()
    peers = sum_peers + y_peers + z_peers + [core_peer] + around
    for peer in peers:
        pl.semaphore_signal(barrier, inc=1, device_id=peer, device_id_type=MESH)
    own_band.wait()
    own_grad.wait()
    for which, held in enumerate((bx.at[0, 1], gs.at[1])):
        for h in range(8):
            at_row = 8 * which + h
            first = held[32 + h * 32 : 48 + h * 32].astype(F32)
            last = held[48 + h * 32 : 64 + h * 32].astype(F32)
            cut[0, at_row : at_row + 1] = first[0:1]
            cut[1, at_row : at_row + 1] = last[15:16]
    strips[...] = cut[...].astype(BF16)
    pl.semaphore_wait(barrier, len(peers))

    started = []

    def send(src, dst, i, peer):
        copy = pltpu.make_async_remote_copy(
            src_ref=src,
            dst_ref=dst,
            send_sem=ssem.at[i],
            recv_sem=rsem.at[i],
            device_id=peer,
            device_id_type=MESH,
        )
        copy.start()
        started.append(copy)
        return copy

    halo = []
    for k, r in enumerate((below, row, above)):
        halo.append(send(strips.at[0], edge.at[1, k], 77 + k, (r, before)))
        halo.append(send(strips.at[1], edge.at[0, k], 80 + k, (r, after)))
    halo.append(send(feat.at[224:256], bx.at[0, 1, 0:32], 83, (below, col)))
    halo.append(send(feat.at[0:32], bx.at[0, 1, 288:320], 84, (above, col)))
    halo.append(send(grad.at[224:256], gs.at[1, 0:32], 85, (below, col)))
    halo.append(send(grad.at[0:32], gs.at[1, 288:320], 86, (above, col)))
    main = {
        d: (
            send(feat, bx.at[d, 1, 32:288], 86 + d, x_peers[d - 1]),
            send(proj, pj.at[d], 89 + d, x_peers[d - 1]),
        )
        for d in (2, 1, 3)
    }
    own_proj.wait()
    ogt[...] = gs[1, 32:288].astype(F32).T.astype(BF16)
    for copy in halo:
        copy.wait_recv()

    def kept(value, outside):
        return jnp.where(outside, jnp.zeros_like(value), value)

    top, bottom = row == 0, row == n_rows - 1
    for held in (bx.at[0, 1], gs.at[1]):
        held[0:32] = kept(held[0:32], top)
        held[288:320] = kept(held[288:320], bottom)
    line[...] = jnp.zeros_like(line)
    for side, outside in enumerate((col == 0, col == n_cols - 1)):
        up, mid, down = [kept(edge[side, k].astype(F32), outside) for k in range(3)]
        for which in range(2):
            rows = 8 * which
            line[which, side, 0:1] = kept(up[rows + 7 : rows + 8], top)
            line[which, side, 1:9] = mid[rows : rows + 8]
            line[which, side, 9:10] = kept(down[rows : rows + 1], bottom)
    be[0] = line[0].astype(BF16)
    ends = {
        d: (
            send(bx.at[0, 1, 0:32], bx.at[d, 1, 0:32], 92 + d, x_peers[d - 1]),
            send(bx.at[0, 1, 288:320], bx.at[d, 1, 288:320], 95 + d, x_peers[d - 1]),
            send(be.at[0], be.at[d], 98 + d, x_peers[d - 1]),
        )
        for d in (2, 1, 3)
    }
    shift_columns(bx, (line[0, 0], line[0, 1]), (0,))

    ci = lax.broadcasted_iota(jnp.int32, (CH, CH), 0)
    to = lax.broadcasted_iota(jnp.int32, (CH, CH), 1)
    source = lax.rem(lax.div(to, 16), NZ) * 64 + lax.div(to, LANES) * 16 + lax.rem(to, 16)
    perm = jnp.where(ci == source, 1.0, 0.0).astype(BF16)
    for b in range(3):
        xsp[b] = dot(bx[0, b], perm).astype(BF16)

    @pl.loop(0, TAPS)
    def _(t):
        start = pl.multiple_of(lax.div(t, 3) * 32, 32)
        terms = dot(ogt[...], xsp[lax.rem(t, 3), pl.ds(start, 256), :]).astype(BF16)
        for yy in range(NY):
            for cc in range(NC):
                first = (yy * NC + cc) * 64
                for xx in range(NX):
                    wt[yy, cc, xx * TAPS + t] = terms[
                        first : first + 64, xx * LANES : (xx + 1) * LANES
                    ]

    core_copy = send(wt.at[:, 1 - core], rc, 0, core_peer)
    shift_columns(gs, (line[1, 0], line[1, 1]), ())

    def sketch_band(slot):
        j = lax.rem(x - slot + NX, NX)
        p = pj[slot]
        for t in range(TAPS):
            a, b = t // 3, t % 3
            part = dot(p, bx[slot, b, a * 32 : a * 32 + 256, :]).astype(BF16)
            for i in range(4):
                q, lane = (4 * t + i) // 9, (4 * t + i) % 9
                m0[j, q, :, lane * LANES : (lane + 1) * LANES] = part[
                    :, i * LANES : (i + 1) * LANES
                ]

    def receive_band(d):
        for copy in main[d] + ends[d]:
            copy.wait_recv()
        edges = be[d].astype(F32)
        shift_columns(bx, (edges[0], edges[1]), (d,))
        sketch_band(d)

    sketch_band(0)
    for d in (3, 1, 2):
        receive_band(d)

    def pair_rows(pair, q):
        return jnp.concatenate([m0[2 * pair, q], m0[2 * pair + 1, q]], axis=0)

    starts = []
    for pair in range(2):
        gram = jnp.zeros((2 * RANK, 2 * RANK), F32)
        for q in range(4):
            stacked = pair_rows(pair, q)
            gram += dot_t(stacked, stacked)
        starts.append(start_spread(gram))
    for pair, combiner in enumerate(combined(starts, mixers[0])):
        for q in range(4):
            m1[pair, q] = dot(combiner, pair_rows(pair, q)).astype(BF16)

    def quarter(q):
        return jnp.concatenate([m1[0, q], m1[1, q]], axis=0)

    gram = jnp.zeros((2 * RANK, 2 * RANK), F32)
    for q in range(4):
        stacked = quarter(q)
        gram += dot_t(stacked, stacked)
    (combiner,) = combined([start_spread(gram)], mixers[0])
    merged = dot(combiner, quarter(x))
    low, high = merged[:, :HALF], merged[:, QUART - HALF :]
    ma[0] = jnp.where(half == 0, low, high).astype(BF16)
    mo[...] = jnp.where(half == 0, high, low).astype(BF16)
    eye = lax.broadcasted_iota(jnp.int32, (RANK, RANK), 0) == lax.broadcasted_iota(
        jnp.int32, (RANK, RANK), 1
    )

    def core_stage():
        core_copy.wait_recv()

        @pl.loop(0, 36)
        def _(i):
            ro[:, i] = (wt[:, core, i].astype(F32) + rc[:, i].astype(F32)).astype(BF16)

        return [
            send(ro.at[lax.rem(y + d, NY)], ry.at[d - 1], d, y_peers[d - 1])
            for d in range(1, NY)
        ]

    def forward():
        weights.wait()
        acc[...] = jnp.zeros_like(acc)

        @pl.loop(0, TAPS)
        def _(t):
            start = pl.multiple_of(lax.div(t, 3) * 32, 32)
            acc[...] += dot(bx[0, lax.rem(t, 3), pl.ds(start, 256), :], kv[t])

        out[...] = acc[...].astype(BF16)

    def backward():
        acc[...] = jnp.zeros_like(acc)

        @pl.loop(0, TAPS)
        def _(t):
            start = pl.multiple_of((2 - lax.div(t, 3)) * 32, 32)
            acc[...] += dot_t(gs[2 - lax.rem(t, 3), pl.ds(start, 256), :], kv[t])

        gfeat[...] = acc[...].astype(BF16)

    def y_stage():
        for copy in y_copies:
            copy.wait_recv()

        @pl.loop(0, 36)
        def _(i):
            total = ro[y, i].astype(F32)
            for d in range(NY - 1):
                total += ry[d, i].astype(F32)
            w2[i] = total.astype(BF16)

        return [
            send(w2.at[pl.ds(lax.rem(x + d, NX) * 9, 9)], rx.at[d - 1], 3 + d, x_peers[d - 1])
            for d in range(1, NX)
        ]

    def x_stage():
        for copy in x_copies:
            copy.wait_recv()
        for pair in range(5):
            halves = []
            for t in (2 * pair, 2 * pair + 1):
                if t < TAPS:
                    total = w2[x * 9 + t].astype(F32)
                    for d in range(NX - 1):
                        total += rx[d, t].astype(F32)
                else:
                    total = jnp.zeros((64, LANES), F32)
                halves.append(total)
            turned = jnp.concatenate(halves, axis=0).T.astype(BF16)
            for k in range(NZ):
                wz[k, pair] = turned[k * 16 : (k + 1) * 16, :]
        return [
            send(wz.at[lax.rem(z + d, NZ)], rz.at[d - 1], 6 + d, z_peers[d - 1])
            for d in range(1, NZ)
        ]

    def flip(value, bit):
        return value + bit - 2 * bit * lax.rem(lax.div(value, bit), 2)

    levels = [
        (at(flip(z, 1), x, y, core), lax.rem(z, 2), 0),
        (at(flip(z, 2), x, y, core), lax.rem(lax.div(z, 2), 2), 0),
        (at(flip(z, 4), x, y, core), lax.div(z, 4), 0),
        (core_peer, core, 1),
        (at(z, x, flip(y, 1), core), lax.rem(y, 2), 1),
        (at(z, x, flip(y, 2), core), lax.div(y, 2), 1),
    ]
    for level, (peer, upper, which) in enumerate(levels):
        base = 14 + 10 * level
        slice_copy = send(mo if level == 0 else ma.at[level], mb.at[level], base, peer)
        within = carried_gram(combiner, gram if level == 0 else gm[...])
        straight = jnp.sum(jnp.where(eye, within, 0.0), axis=0, keepdims=True)
        va[level] = jnp.broadcast_to(straight, (8, RANK))
        da[level] = jnp.where(eye, 0.0, within).astype(BF16)
        gram_copies = [
            send(va.at[level], vb.at[level], base + 1, peer),
            send(da.at[level], db.at[level], base + 2, peer),
        ]
        if level == 0:
            y_copies = core_stage()
        if level == 1:
            forward()
        if level == 2:
            backward()
            x_copies = y_stage()
        if level == 4:
            z_copies = x_stage()
        mix = mixers[which]
        mix = jnp.where(
            upper == 0, mix, jnp.concatenate([mix[:, RANK:], mix[:, :RANK]], axis=1)
        )
        slice_copy.wait_recv()
        shared = 2 * HALF - QUART
        first = dot_t(ma[level, :, :shared], mb[level, :, :shared])
        cross = dot_t(ma[level, :, shared:], mb[level, :, shared:])
        cross = (cross + jnp.where(half == 0, first, 0.0)).astype(BF16)
        po[level] = cross
        cross_copies = [
            send(po.at[level], pr.at[level, k], base + 3 + k, peer)
            for k, peer in sorted(enumerate(sum_peers), key=lambda item: FAR_FIRST[item[0]])
        ]
        for copy in gram_copies:
            copy.wait_recv()
        trace = jnp.sum(va[level, 0:1] + vb[level, 0:1], keepdims=True) + 1e-06
        squared_norm = jnp.zeros((1, 1), F32)
        for k, (straight, rest) in enumerate(((va, da), (vb, db))):
            part = slice(k * RANK, (k + 1) * RANK)
            within = jnp.where(eye, straight[level, 0:1], rest[level].astype(F32))
            gm[part, part] = within
            within = within / trace - jnp.where(eye, 0.5 / RANK, 0.0)
            ym[part, part] = within
            squared_norm += jnp.sum(within * within, keepdims=True)
        for copy in cross_copies:
            copy.wait_recv()
        cross = cross.astype(F32)
        for k in range(NX - 1):
            cross += pr[level, k].astype(F32)
        others = pr[level, NX - 1].astype(F32)
        for k in range(NX, len(sum_peers)):
            others += pr[level, k].astype(F32)
        cross += others.T if level == 0 else others
        scaled = cross / trace
        ym[0:RANK, RANK:] = scaled
        ym[RANK:, 0:RANK] = scaled.T
        squared_norm += 2.0 * jnp.sum(scaled * scaled, keepdims=True)
        (combiner,) = combined([(ym[...], squared_norm)], mix)
        stacked = jnp.concatenate([ma[level], mb[level]], axis=0)
        ma[level + 1] = dot(combiner, stacked).astype(BF16)
        gm[0:RANK, RANK:] = cross
        gm[RANK:, 0:RANK] = cross.T

    last = len(levels)
    own_rows = pl.ds(pl.multiple_of(col * 16, 16), 16)
    fr[0] = ma[last, own_rows, :]
    final_copies = [
        send(ma.at[last, own_rows], fr.at[d], 73 + d, x_peers[d - 1]) for d in range(1, NX)
    ]
    for copy in z_copies:
        copy.wait_recv()
    for pair in range(5):
        total = wz[z, pair].astype(F32)
        for d in range(NZ - 1):
            total += rz[d, pair].astype(F32)
        gk[2 * pair] = total[:, :64]
        if 2 * pair + 1 < TAPS:
            gk[2 * pair + 1] = total[:, 64:]
    for copy in final_copies:
        copy.wait_recv()
    k = lax.broadcasted_iota(jnp.int32, (HALF, 144), 0)
    j = lax.broadcasted_iota(jnp.int32, (HALF, 144), 1)
    skip = lax.rem(row, 8) * 144 - half * (QUART - HALF)
    chosen = jnp.where(k == j + skip, 1.0, 0.0).astype(BF16)
    held = fr[lax.rem(x - lax.div(z, 2) + NX, NX)]
    sketch[...] = dot(held, chosen).astype(BF16)
    for copy in started:
        copy.wait_send()


def step_call(feat, grad, kern, proj, mixers):
    vmem = pl.BlockSpec(memory_space=pltpu.VMEM)
    return pl.pallas_call(
        step_kernel,
        in_specs=[pl.BlockSpec(memory_space=pl.ANY)] * 4 + [vmem],
        out_specs=[vmem] * 4,
        out_shape=[
            pltpu.VMEM((256, CH), BF16),
            pltpu.VMEM((256, CH), BF16),
            pltpu.VMEM((TAPS, 16, 64), F32),
            pltpu.VMEM((16, 144), BF16),
        ],
        scratch_shapes=[
            pltpu.VMEM((NX, 3, 320, CH), BF16),
            pltpu.VMEM((NX, 2, 16, CH), BF16),
            pltpu.VMEM((NX, RANK, 256), BF16),
            pltpu.VMEM((3, 320, CH), BF16),
            pltpu.VMEM((2, 16, CH), BF16),
            pltpu.VMEM((2, 16, CH), F32),
            pltpu.VMEM((2, 3, 16, CH), BF16),
            pltpu.VMEM((2, 2, 16, CH), F32),
            pltpu.VMEM((3, 320, CH), BF16),
            pltpu.VMEM((CH, 256), BF16),
            pltpu.VMEM((TAPS, CH, CH), BF16),
            pltpu.VMEM((NY, NC, 36, 64, LANES), BF16),
            pltpu.VMEM((256, CH), F32),
            pltpu.VMEM((NY, 36, 64, LANES), BF16),
            pltpu.VMEM((NY, 36, 64, LANES), BF16),
            pltpu.VMEM((NY - 1, 36, 64, LANES), BF16),
            pltpu.VMEM((36, 64, LANES), BF16),
            pltpu.VMEM((NX - 1, 9, 64, LANES), BF16),
            pltpu.VMEM((NZ, 5, 16, LANES), BF16),
            pltpu.VMEM((NZ - 1, 5, 16, LANES), BF16),
            pltpu.VMEM((4, 4, RANK, QUART), BF16),
            pltpu.VMEM((2, 4, RANK, QUART), BF16),
            pltpu.VMEM((RANK, HALF), BF16),
            pltpu.VMEM((7, RANK, HALF), BF16),
            pltpu.VMEM((6, RANK, HALF), BF16),
            pltpu.VMEM((6, RANK, RANK), BF16),
            pltpu.VMEM((6, RANK, RANK), BF16),
            pltpu.VMEM((6, 8, RANK), F32),
            pltpu.VMEM((6, 8, RANK), F32),
            pltpu.VMEM((6, RANK, RANK), BF16),
            pltpu.VMEM((6, 7, RANK, RANK), BF16),
            pltpu.VMEM((4, 16, HALF), BF16),
            pltpu.VMEM((2 * RANK, 2 * RANK), F32),
            pltpu.VMEM((2 * RANK, 2 * RANK), F32),
            pltpu.SemaphoreType.DMA((4,)),
            pltpu.SemaphoreType.DMA((102,)),
            pltpu.SemaphoreType.DMA((102,)),
        ],
        compiler_params=pltpu.CompilerParams(
            collective_id=0, has_side_effects=True, vmem_limit_bytes=56 << 20
        ),
        name="conv_step",
    )(feat, grad, kern, proj, mixers)


def settle_kernel(*refs):
    for held, result in zip(refs[:4], refs[4:]):
        result[...] = held[...]


def settle(results):
    vmem = [pl.BlockSpec(memory_space=pltpu.VMEM)] * 4
    return pl.pallas_call(
        settle_kernel,
        in_specs=vmem,
        out_specs=vmem,
        out_shape=[jax.ShapeDtypeStruct(r.shape, r.dtype) for r in results],
        name="results",
    )(*[pltpu.with_memory_space_constraint(r, pltpu.VMEM) for r in results])


def body(features, kernel, out_grad, projector, mixers):
    shape = features.shape
    channels = shape[2]
    results = step_call(
        features.reshape(-1, channels),
        out_grad.reshape(-1, channels),
        kernel.reshape(TAPS, channels, channels),
        projector,
        mixers,
    )
    output, grad_features, grad_kernel, own_block = settle(results)
    return (output.reshape(shape), grad_features.reshape(shape), grad_kernel, own_block)


def solution(mesh):
    in_specs = (P("rows", "cols", None), P(), P("rows", "cols", None), P("rows", "cols"), P())
    out_specs = (
        P("rows", "cols", None),
        P("rows", "cols", None),
        P(None, "rows", "cols"),
        P("cols", "rows"),
    )
    return jax.shard_map(body, mesh=mesh, in_specs=in_specs, out_specs=out_specs, check_vma=False)
```
